256 devices in a mesh: expert: 32 (over z, x), dp: 4 (over y_lo, core), tensor: 2 (over y_hi).
Axes of the slice: x: 4, y: 4 (y_hi: 2, y_lo: 2; y = y_hi * 2 + y_lo), z: 8, core: 2. Of those that a mesh axis runs over, the one named last changes fastest.
Arguments:
- tokens: bfloat16 [24576, 3584], P(('expert', 'dp'), 'tensor'), may hold values from -6 to 6
- routes: int32 [24576, 8], P(('expert', 'dp')), may hold values from 0 to 255, all different within a row
- gates: bfloat16 [24576, 8], P(('expert', 'dp')), may hold values from 0.049804688 to 1
- cotangent: bfloat16 [24576, 3584], P(('expert', 'dp'), 'tensor'), may hold values from -6 to 6
- placement: int32 [32], replicated, may hold values from 0 to 31, each once
- swap_flag: int32 [32], replicated, may hold values from 0 to 1, as said below
- w_gate: bfloat16 [32, 3584, 1024], P('expert', 'dp', 'tensor'), may hold values from -0.09375 to 0.09375
- w_up: bfloat16 [32, 3584, 1024], P('expert', 'dp', 'tensor'), may hold values from -0.09375 to 0.09375
- w_down: bfloat16 [32, 3584, 1024], P('expert', 'dp', 'tensor'), may hold values from -0.1875 to 0.1875
Outputs:
- layer_out: bfloat16 [24576, 3584], P(('expert', 'dp'), 'tensor')
- input_grad: bfloat16 [24576, 3584], P(('expert', 'dp'), 'tensor')
- gate_grad: float32 [24576, 8], P(('expert', 'dp'))
- grad_gate_w: bfloat16 [32, 3584, 1024], P('expert', 'dp', 'tensor')
- grad_up_w: bfloat16 [32, 3584, 1024], P('expert', 'dp', 'tensor')
- grad_down_w: bfloat16 [32, 3584, 1024], P('expert', 'dp', 'tensor')
The draws below stay inside these ranges and needn't reach their ends.
Inputs may be any that keep to these rules, and one draw needn't show every extreme that they name: `swap_flag`: entry i equals entry (i + 16) mod 32; some pair has 1 and some pair 0. `placement`: a permutation of the positions. `routes`: each row names 8 different experts.
All inputs are finite; a program needn't handle non-finite values.
Results may differ from the reference program's by a relative error of at most 0.0095.
Values may be sent and summed in bfloat16 or wider, within the bound.
A program may use at most 128 MiB of HBM per device.

```python
import math
import jax
import jax.numpy as jnp
from jax import lax

D = 3584
HID = 1024
ROUTED = 256
TOPK = 8
TOK_DEV = 192
CAP = 9
TOKENS = 24576
N_EXPERT = 32
N_DP = 4
N_TENSOR = 2


def draw_swap_flag(key, part):
    pairs = N_EXPERT // 2
    first, second, third = jax.random.split(key, 3)
    flags = jax.random.randint(first, (pairs,), 0, 2)
    chosen = jax.random.randint(second, (), 0, pairs)
    other = (chosen + 1 + jax.random.randint(third, (), 0, pairs - 1)) % pairs
    flags = flags.at[chosen].set(1).at[other].set(0)
    return jnp.concatenate([flags, flags]).astype(jnp.int32)


def shard_levels(key, dims, pieces, least, high):
    factor_of, own = 1.0, jax.random.fold_in(key, 6)
    for position, shards_of in pieces:
        draws = jnp.exp(jax.random.uniform(jax.random.fold_in(own, position), (shards_of,), jnp.float32, least / len(pieces), high / len(pieces)))
        factor_of = factor_of * jnp.repeat(draws, dims[position] // shards_of).reshape([-1 if axis == position else 1 for axis in range(len(dims))])
    return factor_of


def different_ones(own_key, rows, amount, top, lift):
    sequence = jax.random.permutation(jax.random.fold_in(own_key, 1), amount)
    favour = sequence
    for power in range(3):
        favour = favour * favour // amount
    favour = favour * lift // amount
    chance = jax.random.randint(jax.random.fold_in(own_key, 2), (rows, amount), 0, 4096) + favour
    fixed_rows = jax.random.permutation(jax.random.fold_in(own_key, 3), rows)[jnp.arange(amount) % rows]
    chance = jnp.where(jnp.arange(rows)[:, None] == fixed_rows[None, :], 1 << 14, chance)
    priority = chance * amount + jnp.arange(amount)
    return lax.top_k(priority.astype(jnp.int32), top)[1].astype(jnp.int32)


def scatter_about(rng, extent, scale, most, cuts=(), kind=jnp.bfloat16):
    level = shard_levels(rng, extent, cuts, -0.22, 0.18) if cuts else 1.0
    entries = jax.random.normal(rng, extent, jnp.float32) * scale * level
    return jnp.minimum(jnp.maximum(entries, -most), most).astype(kind)


def setup_inputs(seed: int = 0) -> dict:
    key_list = jax.random.split(jax.random.key(seed), 10)
    return {
        "tokens": scatter_about(key_list[0], (TOKENS, D), 1.0, 6.0, ((0, 128), (1, 2))),
        "routes": different_ones(key_list[1], TOKENS, ROUTED, TOPK, 512),
        "gates": jnp.clip(jnp.exp(math.log(1.0) - 2.9996462 * jax.random.uniform(key_list[2], (TOKENS, TOPK), jnp.float32) ** shard_levels(key_list[2], (TOKENS, TOPK), ((0, 128),), -0.2, 0.2)), 0.049804688, 1.0).astype(jnp.bfloat16),
        "cotangent": scatter_about(key_list[3], (TOKENS, D), 1.0, 6.0, ((0, 128), (1, 2))),
        "placement": jax.random.permutation(key_list[4], N_EXPERT).astype(jnp.int32),
        "swap_flag": draw_swap_flag(jax.random.fold_in(key_list[9], 71), 0),
        "w_gate": scatter_about(key_list[6], (N_EXPERT, D, HID), D ** -0.5, 0.09375, ((0, 32), (1, 4), (2, 2))),
        "w_up": scatter_about(key_list[7], (N_EXPERT, D, HID), D ** -0.5, 0.09375, ((0, 32), (1, 4), (2, 2))),
        "w_down": scatter_about(key_list[8], (N_EXPERT, D, HID), HID ** -0.5, 0.1875, ((0, 32), (1, 4), (2, 2))),
    }


def rounded(value):
    return lax.optimization_barrier(value.astype(jnp.bfloat16)).astype(jnp.float32)


def reference(tokens, routes, gates, cotangent, placement, swap_flag, w_gate, w_up, w_down):
    experts = N_EXPERT
    places = jnp.arange(experts, dtype=jnp.int32)
    source = jnp.where(swap_flag == 1, (places + experts // 2) % experts, places)
    held = placement[source]
    gate_w = w_gate[source]
    up_w = w_up[source]
    down_w = w_down[source]
    owner_of = jnp.zeros((experts,), jnp.int32).at[held].set(places)
    inside = routes < experts
    owner = jnp.where(inside, owner_of[jnp.where(inside, routes, 0)], experts)
    groups = TOKENS // TOK_DEV
    group_pairs = TOK_DEV * TOPK
    owner_g = owner.reshape(groups, group_pairs)
    onehot = (owner_g[:, :, None] == places[None, None, :]).astype(jnp.int32)
    earlier = jnp.cumsum(onehot, axis=1) - onehot
    slot = jnp.sum(earlier * onehot, axis=2)
    kept = (owner_g < experts) & (slot < CAP)
    group_ids = jnp.broadcast_to(jnp.arange(groups, dtype=jnp.int32)[:, None], (groups, group_pairs))
    sender = group_ids // N_DP
    replica = group_ids % N_DP
    pair_ids = jnp.arange(TOKENS * TOPK, dtype=jnp.int32).reshape(groups, group_pairs)
    rows = experts * CAP
    table = jnp.full((experts, N_DP, rows), -1, jnp.int32)
    table = table.at[jnp.where(kept, owner_g, experts), replica, sender * CAP + jnp.minimum(slot, CAP - 1)].set(pair_ids, mode="drop")
    gate_flat = gates.reshape(-1)
    width = HID // N_TENSOR
    contract = (((0,), (0,)), ((), ()))
    inner = (((1,), (1,)), ((), ()))

    def per_expert(item):
        gate_e, up_e, down_e, tab = item
        outs_eo = []
        outs_dx = []
        outs_dg = []
        grad_g = jnp.zeros((D, HID), jnp.float32)
        grad_u = jnp.zeros((D, HID), jnp.float32)
        grad_d = jnp.zeros((D, HID), jnp.float32)
        for index in range(N_DP):
            pid = tab[index]
            live = pid >= 0
            safe = jnp.where(live, pid, 0)
            token_row = safe // TOPK
            inputs = jnp.where(live[:, None], tokens[token_row], jnp.zeros((), jnp.bfloat16))
            weight = jnp.where(live, gate_flat[safe], jnp.zeros((), jnp.bfloat16)).astype(jnp.float32)
            back = jnp.where(live[:, None], cotangent[token_row], jnp.zeros((), jnp.bfloat16)).astype(jnp.float32)
            pre_gate = jnp.dot(inputs, gate_e, preferred_element_type=jnp.float32)
            pre_up = jnp.dot(inputs, up_e, preferred_element_type=jnp.float32)
            sig = jax.nn.sigmoid(pre_gate)
            hidden = (pre_gate * sig * pre_up).astype(jnp.bfloat16)
            expert_out = jnp.zeros((rows, D), jnp.float32)
            for part in range(N_TENSOR):
                lo_col = part * width
                term = lax.dot_general(hidden[:, lo_col:lo_col + width], down_e[:, lo_col:lo_col + width], inner, preferred_element_type=jnp.float32)
                expert_out = expert_out + rounded(term)
            expert_out = expert_out.astype(jnp.bfloat16)
            outs_dg.append(jnp.sum(back * expert_out.astype(jnp.float32), axis=1))
            d_out = (weight[:, None] * back).astype(jnp.bfloat16)
            d_hidden = jnp.dot(d_out, down_e, preferred_element_type=jnp.float32)
            d_pre_gate = (d_hidden * pre_up * sig * (1.0 + pre_gate * (1.0 - sig))).astype(jnp.bfloat16)
            d_pre_up = (d_hidden * pre_gate * sig).astype(jnp.bfloat16)
            d_inputs = jnp.zeros((rows, D), jnp.float32)
            for part in range(N_TENSOR):
                lo_col = part * width
                term = lax.dot_general(d_pre_gate[:, lo_col:lo_col + width], gate_e[:, lo_col:lo_col + width], inner, preferred_element_type=jnp.float32)
                term = term + lax.dot_general(d_pre_up[:, lo_col:lo_col + width], up_e[:, lo_col:lo_col + width], inner, preferred_element_type=jnp.float32)
                d_inputs = d_inputs + rounded(term)
            outs_eo.append(expert_out)
            outs_dx.append(d_inputs.astype(jnp.bfloat16))
            grad_g = grad_g + rounded(lax.dot_general(inputs, d_pre_gate, contract, preferred_element_type=jnp.float32))
            grad_u = grad_u + rounded(lax.dot_general(inputs, d_pre_up, contract, preferred_element_type=jnp.float32))
            grad_d = grad_d + rounded(lax.dot_general(d_out, hidden, contract, preferred_element_type=jnp.float32))
        return (jnp.stack(outs_eo), jnp.stack(outs_dx), jnp.stack(outs_dg), grad_g.astype(jnp.bfloat16), grad_u.astype(jnp.bfloat16), grad_d.astype(jnp.bfloat16))

    eo_all, dx_all, dg_all, grad_gate_w, grad_up_w, grad_down_w = lax.map(per_expert, (gate_w, up_w, down_w, table))
    pid = table.reshape(-1)
    live = pid >= 0
    token_index = jnp.where(live, pid // TOPK, TOKENS)
    weight_all = jnp.where(live, gate_flat[jnp.where(live, pid, 0)], jnp.zeros((), jnp.bfloat16)).astype(jnp.float32)
    layer_out = jnp.zeros((TOKENS, D), jnp.float32).at[token_index].add(weight_all[:, None] * eo_all.reshape(-1, D).astype(jnp.float32), mode="drop")
    input_grad = jnp.zeros((TOKENS, D), jnp.float32).at[token_index].add(dx_all.reshape(-1, D).astype(jnp.float32), mode="drop")
    gate_grad = jnp.zeros((TOKENS * TOPK,), jnp.float32).at[jnp.where(live, pid, TOKENS * TOPK)].set(dg_all.reshape(-1), mode="drop").reshape(TOKENS, TOPK)
    return (layer_out.astype(jnp.bfloat16), input_grad.astype(jnp.bfloat16), gate_grad, grad_gate_w, grad_up_w, grad_down_w)
```

```python
import jax
import jax.numpy as jnp
from jax import lax
from jax.sharding import PartitionSpec as P

CAP = 9


def swapped(block, axis, stride):
    count = lax.axis_size(axis)
    route = []
    for low in range(count):
        high = low | 1 << stride
        if high != low and high < count:
            route += [(low, high), (high, low)]
    return lax.ppermute(block, axis, route)


def on_device(tokens, routes, gates, cotangent, placement, swap_flag, w_gate, w_up, w_down):
    experts = lax.axis_size("expert")
    myself = lax.axis_index("expert")
    bit_high = experts.bit_length() - 2
    places = jnp.arange(experts, dtype=jnp.int32)
    partner = (places + experts // 2) % experts
    source = jnp.where(swap_flag == 1, partner, places)
    my_flag = jnp.sum(jnp.where(places == myself, swap_flag, 0)) == 1
    own = (w_gate[0], w_up[0], w_down[0])
    moved = swapped((w_gate[0], w_up[0], w_down[0]), "expert", bit_high)
    local_w = tuple((jnp.where(my_flag, fresh, former) for fresh, former in zip(moved, own)))
    held = jnp.sum(jnp.where(source[:, None] == places[None, :], placement[None, :], 0), axis=1)
    gate_full, up_full, down_full = (
        lax.all_gather(local_w[0], "dp", axis=0, tiled=True),
        lax.all_gather(local_w[1], "dp", axis=0, tiled=True),
        lax.all_gather(local_w[2], "dp", axis=0, tiled=True),
    )
    tok_count, top_count = routes.shape
    slots_all = experts * CAP
    pair_owner = routes[:, :, None] == held[None, None, :]
    named = jnp.any(pair_owner, axis=1)
    gate_of = jnp.sum(jnp.where(pair_owner, gates[:, :, None].astype(jnp.float32), 0.0), axis=1)
    before = jnp.arange(tok_count)[:, None] > jnp.arange(tok_count)[None, :]
    earlier = jnp.dot(
        before.astype(jnp.bfloat16), named.astype(jnp.bfloat16), preferred_element_type=jnp.float32
    ).astype(jnp.int32)
    rank = jnp.where(named, earlier, CAP)
    match = rank[:, :, None] == jnp.arange(CAP, dtype=jnp.int32)[None, None, :]
    select = match.astype(jnp.bfloat16).reshape(tok_count, slots_all)
    weighted = (
        jnp.where(match, gate_of[:, :, None], 0.0).astype(jnp.bfloat16).reshape(tok_count, slots_all)
    )
    half_width = tokens.shape[1]
    contract = (((0,), (0,)), ((), ()))
    inner = (((1,), (1,)), ((), ()))
    outgoing = lax.dot_general(select, tokens, contract, preferred_element_type=jnp.float32).astype(
        jnp.bfloat16
    )
    arrived = lax.all_to_all(
        outgoing.reshape(experts, CAP, half_width),
        "expert",
        split_axis=0,
        concat_axis=0,
        tiled=True,
    )
    expert_in = lax.all_gather(arrived.reshape(slots_all, half_width), "tensor", axis=1, tiled=True)
    pre_gate = jnp.dot(expert_in, gate_full, preferred_element_type=jnp.float32)
    pre_up = jnp.dot(expert_in, up_full, preferred_element_type=jnp.float32)
    sig = jax.nn.sigmoid(pre_gate)
    hidden = (pre_gate * sig * pre_up).astype(jnp.bfloat16)
    out_terms = lax.dot_general(hidden, down_full, inner, preferred_element_type=jnp.float32)
    out_half = lax.psum_scatter(
        out_terms.astype(jnp.bfloat16), "tensor", scatter_dimension=1, tiled=True
    )
    returned = lax.all_to_all(
        out_half.reshape(experts, CAP, half_width),
        "expert",
        split_axis=0,
        concat_axis=0,
        tiled=True,
    ).reshape(slots_all, half_width)
    layer_out = jnp.dot(weighted, returned, preferred_element_type=jnp.float32).astype(jnp.bfloat16)
    scores = lax.dot_general(cotangent, returned, inner, preferred_element_type=jnp.float32)
    owner_score = jnp.sum(
        jnp.where(match, scores.reshape(tok_count, experts, CAP), 0.0), axis=2
    )
    gate_part = jnp.sum(jnp.where(pair_owner, owner_score[:, None, :], 0.0), axis=2)
    gate_grad = lax.psum(gate_part, "tensor")
    d_outgoing = lax.dot_general(
        weighted, cotangent, contract, preferred_element_type=jnp.float32
    ).astype(jnp.bfloat16)
    d_arrived = lax.all_to_all(
        d_outgoing.reshape(experts, CAP, half_width),
        "expert",
        split_axis=0,
        concat_axis=0,
        tiled=True,
    )
    d_out = lax.all_gather(d_arrived.reshape(slots_all, half_width), "tensor", axis=1, tiled=True)
    d_hidden = jnp.dot(d_out, down_full, preferred_element_type=jnp.float32)
    d_pre_gate = (d_hidden * pre_up * sig * (1.0 + pre_gate * (1.0 - sig))).astype(jnp.bfloat16)
    d_pre_up = (d_hidden * pre_gate * sig).astype(jnp.bfloat16)
    in_terms = lax.dot_general(d_pre_gate, gate_full, inner, preferred_element_type=jnp.float32)
    in_terms = in_terms + lax.dot_general(
        d_pre_up, up_full, inner, preferred_element_type=jnp.float32
    )
    in_half = lax.psum_scatter(
        in_terms.astype(jnp.bfloat16), "tensor", scatter_dimension=1, tiled=True
    )
    back_rows = lax.all_to_all(
        in_half.reshape(experts, CAP, half_width), "expert", split_axis=0, concat_axis=0, tiled=True
    ).reshape(slots_all, half_width)
    input_grad = jnp.dot(select, back_rows, preferred_element_type=jnp.float32).astype(jnp.bfloat16)
    units = hidden.shape[1]
    summed = lax.psum_scatter(
        jnp.concatenate(
            [
                lax.dot_general(
                    expert_in, d_pre_gate, contract, preferred_element_type=jnp.float32
                ),
                lax.dot_general(expert_in, d_pre_up, contract, preferred_element_type=jnp.float32),
                lax.dot_general(d_out, hidden, contract, preferred_element_type=jnp.float32),
            ],
            axis=1,
        ).astype(jnp.bfloat16),
        "dp",
        scatter_dimension=0,
        tiled=True,
    )
    grads = (
        summed[:, :units][None],
        summed[:, units : 2 * units][None],
        summed[:, 2 * units :][None],
    )
    return (layer_out, input_grad, gate_grad, grads[0], grads[1], grads[2])


def solution(mesh):
    placed = (
        P(("expert", "dp"), "tensor"),
        P(("expert", "dp"), None),
        P(("expert", "dp"), None),
        P(("expert", "dp"), "tensor"),
        P(),
        P(),
        P("expert", "dp", "tensor"),
        P("expert", "dp", "tensor"),
        P("expert", "dp", "tensor"),
    )
    return jax.shard_map(
        on_device,
        mesh=mesh,
        in_specs=placed,
        out_specs=(
            P(("expert", "dp"), "tensor"),
            P(("expert", "dp"), "tensor"),
            P(("expert", "dp"), None),
            P("expert", "dp", "tensor"),
            P("expert", "dp", "tensor"),
            P("expert", "dp", "tensor"),
        ),
        check_vma=False,
    )
```

```python
import functools

import jax
import jax.numpy as jnp
from jax import lax
from jax.experimental import pallas as pl
from jax.experimental.pallas import tpu as pltpu
from jax.sharding import PartitionSpec as P

CAP = 9
TILE = 8
LANES = 128
MESH = pl.DeviceIdType.MESH


def exchange_kernel(experts, main, rest, main_out, rest_out, local, sent, got, sent_rest, got_rest):
    me = lax.axis_index("expert")
    barrier = pltpu.get_barrier_semaphore()

    def greet(step, carry):
        pl.semaphore_signal(
            barrier, inc=1, device_id={"expert": (me + step) % experts}, device_id_type=MESH
        )
        return carry

    lax.fori_loop(1, experts, greet, 0)
    pl.semaphore_wait(barrier, experts - 1)

    def rows(which):
        return pl.ds(pl.multiple_of(which * TILE, TILE), TILE)

    def copies(step):
        peer = (me + step) % experts
        return (
            pltpu.make_async_remote_copy(
                main.at[rows(peer)],
                main_out.at[rows(me)],
                sent.at[step],
                got.at[step],
                device_id={"expert": peer},
                device_id_type=MESH,
            ),
            pltpu.make_async_remote_copy(
                rest.at[peer],
                rest_out.at[me],
                sent_rest.at[step],
                got_rest.at[step],
                device_id={"expert": peer},
                device_id_type=MESH,
            ),
        )

    def begin(step, carry):
        for copy in copies(step):
            copy.start()
        return carry

    def finish(step, carry):
        for copy in copies(step):
            copy.wait()
        return carry

    own_main = pltpu.make_async_copy(main.at[rows(me)], main_out.at[rows(me)], local.at[0])
    own_rest = pltpu.make_async_copy(rest.at[me], rest_out.at[me], local.at[1])
    own_main.start()
    own_rest.start()
    lax.fori_loop(1, experts, begin, 0)
    lax.fori_loop(1, experts, finish, 0)
    own_main.wait()
    own_rest.wait()


def exchanged(block, identity):
    experts = lax.axis_size("expert")
    count, width = block.shape
    main = block[: experts * TILE]
    rest = block[experts * TILE :].reshape(experts, width // LANES, LANES)
    any_space = pl.BlockSpec(memory_space=pl.ANY)
    main, rest = pl.pallas_call(
        functools.partial(exchange_kernel, experts),
        name=f"exchange_{identity}",
        out_shape=(
            jax.ShapeDtypeStruct(main.shape, main.dtype),
            jax.ShapeDtypeStruct(rest.shape, rest.dtype),
        ),
        in_specs=[any_space] * 2,
        out_specs=(any_space, any_space),
        scratch_shapes=[pltpu.SemaphoreType.DMA((2,))]
        + [pltpu.SemaphoreType.DMA((experts,))] * 4,
        compiler_params=pltpu.CompilerParams(collective_id=identity, has_side_effects=True),
    )(main, rest)
    return jnp.concatenate([main, rest.reshape(experts, width)], axis=0)


def swapped(block, axis, stride):
    count = lax.axis_size(axis)
    route = []
    for low in range(count):
        high = low | 1 << stride
        if high != low and high < count:
            route += [(low, high), (high, low)]
    return lax.ppermute(block, axis, route)


def on_device(tokens, routes, gates, cotangent, placement, swap_flag, w_gate, w_up, w_down):
    experts = lax.axis_size("expert")
    myself = lax.axis_index("expert")
    bit_high = experts.bit_length() - 2
    places = jnp.arange(experts, dtype=jnp.int32)
    partner = (places + experts // 2) % experts
    source = jnp.where(swap_flag == 1, partner, places)
    my_flag = jnp.sum(jnp.where(places == myself, swap_flag, 0)) == 1
    own = (w_gate[0], w_up[0], w_down[0])
    moved = swapped((w_gate[0], w_up[0], w_down[0]), "expert", bit_high)
    local_w = tuple((jnp.where(my_flag, fresh, former) for fresh, former in zip(moved, own)))
    held = jnp.sum(jnp.where(source[:, None] == places[None, :], placement[None, :], 0), axis=1)
    gate_full, up_full, down_full = (
        lax.all_gather(local_w[0], "dp", axis=0, tiled=True),
        lax.all_gather(local_w[1], "dp", axis=0, tiled=True),
        lax.all_gather(local_w[2], "dp", axis=0, tiled=True),
    )
    tok_count, top_count = routes.shape
    slots_all = experts * CAP
    pair_owner = routes[:, :, None] == held[None, None, :]
    named = jnp.any(pair_owner, axis=1)
    gate_of = jnp.sum(jnp.where(pair_owner, gates[:, :, None].astype(jnp.float32), 0.0), axis=1)
    before = jnp.arange(tok_count)[:, None] > jnp.arange(tok_count)[None, :]
    earlier = jnp.dot(
        before.astype(jnp.bfloat16), named.astype(jnp.bfloat16), preferred_element_type=jnp.float32
    ).astype(jnp.int32)
    rank = jnp.where(named, earlier, CAP)
    column = jnp.arange(slots_all, dtype=jnp.int32)
    in_main = column < experts * TILE
    column_owner = jnp.where(in_main, column // TILE, column - experts * TILE)
    column_slot = jnp.where(in_main, column % TILE, TILE)
    spread = (places[:, None] == column_owner[None, :]).astype(jnp.bfloat16)
    column_rank = jnp.dot(rank.astype(jnp.bfloat16), spread, preferred_element_type=jnp.float32)
    match = column_rank == column_slot[None, :].astype(jnp.float32)
    select = match.astype(jnp.bfloat16)
    column_gate = jnp.dot(gate_of.astype(jnp.bfloat16), spread, preferred_element_type=jnp.float32)
    weighted = jnp.where(match, column_gate, 0.0).astype(jnp.bfloat16)
    contract = (((0,), (0,)), ((), ()))
    inner = (((1,), (1,)), ((), ()))
    outgoing = lax.dot_general(select, tokens, contract, preferred_element_type=jnp.float32).astype(
        jnp.bfloat16
    )
    expert_in = lax.all_gather(exchanged(outgoing, 0), "tensor", axis=1, tiled=True)
    pre_gate = jnp.dot(expert_in, gate_full, preferred_element_type=jnp.float32)
    pre_up = jnp.dot(expert_in, up_full, preferred_element_type=jnp.float32)
    sig = jax.nn.sigmoid(pre_gate)
    hidden = (pre_gate * sig * pre_up).astype(jnp.bfloat16)
    out_terms = lax.dot_general(hidden, down_full, inner, preferred_element_type=jnp.float32)
    out_half = lax.psum_scatter(
        out_terms.astype(jnp.bfloat16), "tensor", scatter_dimension=1, tiled=True
    )
    returned = exchanged(out_half, 1)
    layer_out = jnp.dot(weighted, returned, preferred_element_type=jnp.float32).astype(jnp.bfloat16)
    scores = lax.dot_general(cotangent, returned, inner, preferred_element_type=jnp.float32)
    owner_score = lax.dot_general(
        jnp.where(match, scores, 0.0),
        spread.astype(jnp.float32),
        inner,
        precision=lax.Precision.HIGHEST,
        preferred_element_type=jnp.float32,
    )
    gate_part = jnp.sum(jnp.where(pair_owner, owner_score[:, None, :], 0.0), axis=2)
    gate_grad = lax.psum(gate_part, "tensor")
    d_outgoing = lax.dot_general(
        weighted, cotangent, contract, preferred_element_type=jnp.float32
    ).astype(jnp.bfloat16)
    d_out = lax.all_gather(exchanged(d_outgoing, 2), "tensor", axis=1, tiled=True)
    d_hidden = jnp.dot(d_out, down_full, preferred_element_type=jnp.float32)
    d_pre_gate = (d_hidden * pre_up * sig * (1.0 + pre_gate * (1.0 - sig))).astype(jnp.bfloat16)
    d_pre_up = (d_hidden * pre_gate * sig).astype(jnp.bfloat16)
    in_terms = lax.dot_general(d_pre_gate, gate_full, inner, preferred_element_type=jnp.float32)
    in_terms = in_terms + lax.dot_general(
        d_pre_up, up_full, inner, preferred_element_type=jnp.float32
    )
    in_half = lax.psum_scatter(
        in_terms.astype(jnp.bfloat16), "tensor", scatter_dimension=1, tiled=True
    )
    back_rows = exchanged(in_half, 3)
    input_grad = jnp.dot(select, back_rows, preferred_element_type=jnp.float32).astype(jnp.bfloat16)
    units = hidden.shape[1]
    summed = lax.psum_scatter(
        jnp.concatenate(
            [
                lax.dot_general(
                    expert_in, d_pre_gate, contract, preferred_element_type=jnp.float32
                ),
                lax.dot_general(expert_in, d_pre_up, contract, preferred_element_type=jnp.float32),
                lax.dot_general(d_out, hidden, contract, preferred_element_type=jnp.float32),
            ],
            axis=1,
        ).astype(jnp.bfloat16),
        "dp",
        scatter_dimension=0,
        tiled=True,
    )
    grads = (
        summed[:, :units][None],
        summed[:, units : 2 * units][None],
        summed[:, 2 * units :][None],
    )
    return (layer_out, input_grad, gate_grad, grads[0], grads[1], grads[2])


def solution(mesh):
    placed = (
        P(("expert", "dp"), "tensor"),
        P(("expert", "dp"), None),
        P(("expert", "dp"), None),
        P(("expert", "dp"), "tensor"),
        P(),
        P(),
        P("expert", "dp", "tensor"),
        P("expert", "dp", "tensor"),
        P("expert", "dp", "tensor"),
    )
    return jax.shard_map(
        on_device,
        mesh=mesh,
        in_specs=placed,
        out_specs=(
            P(("expert", "dp"), "tensor"),
            P(("expert", "dp"), "tensor"),
            P(("expert", "dp"), None),
            P("expert", "dp", "tensor"),
            P("expert", "dp", "tensor"),
            P("expert", "dp", "tensor"),
        ),
        check_vma=False,
    )
```

```python
import functools

import jax
import jax.numpy as jnp
from jax import lax
from jax.experimental import pallas as pl
from jax.experimental.pallas import tpu as pltpu
from jax.sharding import PartitionSpec as P

CAP = 9
TILE = 8
LANES = 128
PARTS = 2
MESH = pl.DeviceIdType.MESH
ANY = pl.BlockSpec(memory_space=pl.ANY)
WHOLE = pl.BlockSpec(memory_space=pltpu.VMEM)


def remote(src, dst, sent, got, where):
    return pltpu.make_async_remote_copy(
        src_ref=src,
        dst_ref=dst,
        send_sem=sent,
        recv_sem=got,
        device_id=where,
        device_id_type=MESH,
    )


def greet(experts, replicas, halves, me, dp, tensor):
    barrier = pltpu.get_barrier_semaphore()
    group = replicas * halves

    def along(step, carry):
        pl.semaphore_signal(
            barrier, inc=1, device_id={"expert": (me + step) % experts}, device_id_type=MESH
        )
        return carry

    def inside(step, carry):
        other = (dp * halves + tensor + step) % group
        pl.semaphore_signal(
            barrier,
            inc=1,
            device_id={"dp": other // halves, "tensor": other % halves},
            device_id_type=MESH,
        )
        return carry

    lax.fori_loop(1, experts, along, 0)
    lax.fori_loop(1, group, inside, 0)
    pl.semaphore_wait(barrier, experts - 1 + group - 1)


def gather_kernel(
    experts, replicas, halves, xm, xr, gm, gr, wg, wu, wd, flag,
    xf, xrf, xs, xrs, gf, grf, gs, grs, wgf, wuf, wdf,
    arriving, held, a2a_sems, row_sems, slice_sems, weight_sems, local_sems,
):
    me, dp, tensor = lax.axis_index("expert"), lax.axis_index("dp"), lax.axis_index("tensor")
    depth, half = wg.shape[0], xm.shape[2]
    piece = depth // PARTS
    own, full = (wg, wu, wd), (wgf, wuf, wdf)
    sibling = {"dp": dp + 1 - 2 * (dp % 2)}
    across = {"dp": (dp + 2) % replicas}
    across_dp = (dp + 2) % replicas
    other_half = 1 - tensor
    greet(experts, replicas, halves, me, dp, tensor)

    columns = pl.ds(pl.multiple_of(tensor * half, LANES), half)
    pairs = pl.ds(tensor * 2, 2)

    def slabs(index, step):
        peer = (me + step) % experts
        main, rest, main_to, rest_to = ((xm, xr, xf, xrf), (gm, gr, gf, grf))[index]
        sems = a2a_sems.at[index]
        return (
            remote(
                main.at[peer], main_to.at[me, :, columns],
                sems.at[0, step], sems.at[1, step], {"expert": peer},
            ),
            remote(
                rest.at[peer], rest_to.at[me, pairs],
                sems.at[2, step], sems.at[3, step], {"expert": peer},
            ),
        )

    def own_slabs(index):
        main, rest, main_to, rest_to = ((xm, xr, xf, xrf), (gm, gr, gf, grf))[index]
        return (
            pltpu.make_async_copy(
                main.at[me], main_to.at[me, :, columns], local_sems.at[2 * index]
            ),
            pltpu.make_async_copy(rest.at[me], rest_to.at[me, pairs], local_sems.at[2 * index + 1]),
        )

    for index in range(2):
        for copy in own_slabs(index):
            copy.start()

        def begin(step, carry, index=index):
            for copy in slabs(index, step):
                copy.start()
            return carry

        lax.fori_loop(1, experts, begin, 0)

    def rows(part):
        return pl.ds(part * piece, piece)

    def swap(matrix, part):
        sems = weight_sems.at[0, matrix, part]
        return remote(
            own[matrix].at[rows(part)], arriving.at[matrix, rows(part)],
            sems.at[0], sems.at[1], {"expert": (me + experts // 2) % experts},
        )

    def stay(matrix):
        return pltpu.make_async_copy(own[matrix], held.at[matrix], local_sems.at[4 + matrix])

    for matrix in range(3):
        stay(matrix).start()
        for part in range(PARTS):
            swap(matrix, part).start()

    def row_copies(index):
        main, rest = ((xf, xrf), (gf, grf))[index]
        sems = row_sems.at[index]
        peer = {"tensor": other_half}
        return (
            remote(main.at[:, :, columns], main.at[:, :, columns], sems.at[0], sems.at[1], peer),
            remote(rest.at[:, pairs], rest.at[:, pairs], sems.at[2], sems.at[3], peer),
        )

    def slice_copies(index, part, stays):
        main, rest, main_to, rest_to = ((xf, xrf, xs, xrs), (gf, grf, gs, grs))[index]
        target = tensor * 2 + part
        width = half // 2
        which = pl.ds(pl.multiple_of(target * width, LANES), width)
        where = {"dp": target, "tensor": tensor if stays else other_half}
        sent = slice_sems.at[index, 0, 2 * part + stays]
        got = slice_sems.at[index, 1, dp]
        return (
            remote(main.at[:, :, which], main_to.at[dp], sent.at[0], got.at[0], where),
            remote(rest.at[:, target], rest_to.at[dp], sent.at[1], got.at[1], where),
        )

    def slice_here(index):
        main, rest, main_to, rest_to = ((xf, xrf, xs, xrs), (gf, grf, gs, grs))[index]
        width = half // 2
        which = pl.ds(pl.multiple_of(dp * width, LANES), width)
        got = slice_sems.at[index, 1, dp]
        return (
            pltpu.make_async_copy(main.at[:, :, which], main_to.at[dp], got.at[0]),
            pltpu.make_async_copy(rest.at[:, dp], rest_to.at[dp], got.at[1]),
        )

    for index in range(2):
        for copy in own_slabs(index):
            copy.wait()

        def arrive(step, carry, index=index):
            for copy in slabs(index, step):
                copy.wait_recv()
            return carry

        lax.fori_loop(1, experts, arrive, 0)
        for copy in row_copies(index):
            copy.start()
        for part in range(2):
            for copy in slice_copies(index, part, 0):
                copy.start()

            @pl.when(dp == tensor * 2 + part)
            def _(index=index):
                for copy in slice_here(index):
                    copy.start()

            @pl.when(dp != tensor * 2 + part)
            def _(index=index, part=part):
                for copy in slice_copies(index, part, 1):
                    copy.start()

    def spread(matrix, part, kind):
        start = across_dp if kind == 2 else dp
        place = pl.ds(pl.multiple_of(start * depth + part * piece, TILE), piece)
        src = full[matrix].at[place] if kind == 2 else held.at[matrix, rows(part)]
        sems = weight_sems.at[1 + kind, matrix, part]
        where = across if kind == 1 else sibling
        return remote(src, full[matrix].at[place], sems.at[0], sems.at[1], where)

    def keep(matrix, part):
        place = pl.ds(pl.multiple_of(dp * depth + part * piece, TILE), piece)
        return pltpu.make_async_copy(
            held.at[matrix, rows(part)],
            full[matrix].at[place],
            local_sems.at[7 + matrix * PARTS + part],
        )

    def forward(matrix, part):
        spread(matrix, part, 1).wait_recv()
        spread(matrix, part, 2).start()

    order = [(matrix, part) for matrix in range(3) for part in range(PARTS)]
    taken = flag[0:1, :]
    for number, (matrix, part) in enumerate(order):
        if part == 0:
            stay(matrix).wait()
        swap(matrix, part).wait_recv()

        def choose(block, carry, matrix=matrix, part=part):
            lines = pl.ds(pl.multiple_of(part * piece + block * 64, 64), 64)
            fresh = arriving[matrix, lines, :].astype(jnp.float32)
            former = held[matrix, lines, :].astype(jnp.float32)
            held[matrix, lines, :] = (fresh * taken + former * (1.0 - taken)).astype(held.dtype)
            return carry

        lax.fori_loop(0, piece // 64, choose, 0)
        spread(matrix, part, 1).start()
        spread(matrix, part, 0).start()
        keep(matrix, part).start()
        if number > 0:
            forward(*order[number - 1])
    forward(*order[-1])

    for matrix, part in order:
        swap(matrix, part).wait_send()
        spread(matrix, part, 1).wait_send()
        spread(matrix, part, 0).wait()
        spread(matrix, part, 2).wait()
        keep(matrix, part).wait()
    for index in range(2):

        def leave(step, carry, index=index):
            for copy in slabs(index, step):
                copy.wait_send()
            return carry

        lax.fori_loop(1, experts, leave, 0)
        for copy in row_copies(index):
            copy.wait()
        for part in range(2):
            for copy in slice_copies(index, part, 0):
                copy.wait_send()

            @pl.when(dp != tensor * 2 + part)
            def _(index=index, part=part):
                for copy in slice_copies(index, part, 1):
                    copy.wait_send()

        main, rest, main_to, rest_to = ((xf, xrf, xs, xrs), (gf, grf, gs, grs))[index]

        def landed(source, carry, index=index, main_to=main_to, rest_to=rest_to):
            got = slice_sems.at[index, 1, source]
            pltpu.make_async_copy(main_to.at[source], main_to.at[source], got.at[0]).wait()
            pltpu.make_async_copy(rest_to.at[source], rest_to.at[source], got.at[1]).wait()
            return carry

        lax.fori_loop(0, replicas, landed, 0)


def gathered(x_rows, g_rows, weights, flag):
    experts, replicas, halves = (lax.axis_size(a) for a in ("expert", "dp", "tensor"))
    half = x_rows.shape[1]
    depth, units = weights[0].shape
    lines = half // 2 // LANES

    def pieces(block):
        main = block[: experts * TILE].reshape(experts, TILE, half)
        rest = block[experts * TILE :].reshape(experts, 2, lines, LANES)
        return main, rest

    def like(*shape):
        return jax.ShapeDtypeStruct(shape, jnp.bfloat16)

    landing = (
        like(experts, TILE, half * halves),
        like(experts, 2 * halves, lines, LANES),
        like(replicas, experts, TILE, half // 2),
        like(replicas, experts, lines, LANES),
    )
    out_shape = landing * 2 + (like(depth * replicas, units),) * 3
    dma = pltpu.SemaphoreType.DMA
    outs = pl.pallas_call(
        functools.partial(gather_kernel, experts, replicas, halves),
        name="gather_all",
        out_shape=out_shape,
        in_specs=[ANY] * 7 + [WHOLE],
        out_specs=(ANY,) * len(out_shape),
        scratch_shapes=[
            pltpu.VMEM((3, depth, units), jnp.bfloat16),
            pltpu.VMEM((3, depth, units), jnp.bfloat16),
            dma((2, 4, experts)),
            dma((2, 4)),
            dma((2, 2, 4, 2)),
            dma((4, 3, PARTS, 2)),
            dma((7 + 3 * PARTS,)),
        ],
        compiler_params=pltpu.CompilerParams(
            collective_id=0, has_side_effects=True, vmem_limit_bytes=24 << 20
        ),
    )(*pieces(x_rows), *pieces(g_rows), *weights, flag)

    def joined(main, rest, lead):
        main = main.reshape(lead + (experts * TILE, -1))
        rest = rest.reshape(lead + (experts, -1))
        return jnp.concatenate([main, rest], axis=len(lead))

    x_full, x_slice = joined(outs[0], outs[1], ()), joined(outs[2], outs[3], (replicas,))
    g_full, g_slice = joined(outs[4], outs[5], ()), joined(outs[6], outs[7], (replicas,))
    return x_full, x_slice, g_full, g_slice, outs[8:]


def return_kernel(
    experts, replicas, halves, om, rest_o, im, rest_i, factors,
    om_to, rest_o_to, im_to, rest_i_to, factors_to,
    own_o, own_ro, own_i, own_ri, got_o, got_ro, got_i, got_ri,
    tensor_sems, back_sems, factor_sems, local_sems,
):
    me, dp, tensor = lax.axis_index("expert"), lax.axis_index("dp"), lax.axis_index("tensor")
    half = om_to.shape[2]
    other_half = 1 - tensor
    sibling = {"dp": dp + 1 - 2 * (dp % 2)}
    across_dp = (dp + 2) % replicas
    greet(experts, replicas, halves, me, dp, tensor)

    def columns(which):
        return pl.ds(pl.multiple_of(which * half, LANES), half)

    sides = (
        (om, rest_o, own_o, own_ro, got_o, got_ro, om_to, rest_o_to),
        (im, rest_i, own_i, own_ri, got_i, got_ri, im_to, rest_i_to),
    )

    def mine(index):
        main, rest, own_main, own_rest = sides[index][:4]
        return (
            pltpu.make_async_copy(
                main.at[:, :, columns(tensor)], own_main, local_sems.at[2 * index]
            ),
            pltpu.make_async_copy(rest.at[tensor], own_rest, local_sems.at[2 * index + 1]),
        )

    def halves_over(index, step):
        main, rest = sides[index][:2]
        got_main, got_rest = sides[index][4:6]
        peer = (me + step) % experts
        sems = tensor_sems.at[index]
        where = {"tensor": other_half}
        return (
            remote(
                main.at[peer, :, columns(other_half)], got_main.at[peer],
                sems.at[0, step], sems.at[1, step], where,
            ),
            remote(
                rest.at[other_half, peer], got_rest.at[peer],
                sems.at[2, step], sems.at[3, step], where,
            ),
        )

    def back(index, step):
        own_main, own_rest = sides[index][2:4]
        main_to, rest_to = sides[index][6:]
        peer = (me + step) % experts
        sems = back_sems.at[index]
        return (
            remote(
                own_main.at[peer], main_to.at[me], sems.at[0, step], sems.at[1, step],
                {"expert": peer},
            ),
            remote(
                own_rest.at[peer], rest_to.at[me], sems.at[2, step], sems.at[3, step],
                {"expert": peer},
            ),
        )

    def back_here(index):
        own_main, own_rest = sides[index][2:4]
        main_to, rest_to = sides[index][6:]
        return (
            pltpu.make_async_copy(own_main.at[me], main_to.at[me], local_sems.at[4 + 2 * index]),
            pltpu.make_async_copy(own_rest.at[me], rest_to.at[me], local_sems.at[5 + 2 * index]),
        )

    def factor(kind):
        which = across_dp if kind == 2 else dp
        src = factors_to.at[which] if kind == 2 else factors
        where = {"dp": across_dp} if kind == 1 else sibling
        return remote(
            src, factors_to.at[which], factor_sems.at[kind, 0], factor_sems.at[kind, 1], where
        )

    factor_here = pltpu.make_async_copy(factors, factors_to.at[dp], local_sems.at[8])
    for index in range(2):
        for copy in mine(index):
            copy.start()

        def begin(step, carry, index=index):
            for copy in halves_over(index, step):
                copy.start()
            return carry

        lax.fori_loop(0, experts, begin, 0)
    factor(1).start()
    factor(0).start()
    factor_here.start()

    for index in range(2):
        for copy in mine(index):
            copy.wait()
        own_main, own_rest, got_main, got_rest = sides[index][2:6]

        def add(step, index=index):
            for copy in halves_over(index, step):
                copy.wait_recv()
            peer = (me + step) % experts
            for own, got in ((own_main, got_main), (own_rest, got_rest)):
                own[peer] = (own[peer].astype(jnp.float32) + got[peer].astype(jnp.float32)).astype(
                    own.dtype
                )

        def pass_on(step, carry, index=index, add=add):
            add(step)
            for copy in back(index, step):
                copy.start()
            return carry

        lax.fori_loop(1, experts, pass_on, 0)
        add(0)
        for copy in back_here(index):
            copy.start()

    factor(1).wait_recv()
    factor(2).start()
    for index in range(2):

        def finish(step, carry, index=index):
            for copy in back(index, step):
                copy.wait()
            return carry

        def sent(step, carry, index=index):
            for copy in halves_over(index, step):
                copy.wait_send()
            return carry

        lax.fori_loop(1, experts, finish, 0)
        lax.fori_loop(0, experts, sent, 0)
        for copy in back_here(index):
            copy.wait()
    factor_here.wait()
    factor(1).wait_send()
    factor(0).wait()
    factor(2).wait()


def given_back(out_terms, in_terms, factors):
    experts, replicas, halves = (lax.axis_size(a) for a in ("expert", "dp", "tensor"))
    half = out_terms.shape[1] // halves
    lines = half // LANES

    def pieces(block):
        main = block[: experts * TILE].reshape(experts, TILE, halves * half)
        rest = block[experts * TILE :].reshape(experts, halves, lines, LANES)
        return main, rest.transpose(1, 0, 2, 3)

    def like(*shape):
        return jax.ShapeDtypeStruct(shape, jnp.bfloat16)

    landing = (like(experts, TILE, half), like(experts, lines, LANES))
    out_shape = landing * 2 + (like(replicas, *factors.shape),)
    dma = pltpu.SemaphoreType.DMA
    keep = [pltpu.VMEM(shape.shape, shape.dtype) for shape in landing]
    outs = pl.pallas_call(
        functools.partial(return_kernel, experts, replicas, halves),
        name="return_all",
        out_shape=out_shape,
        in_specs=[ANY] * 5,
        out_specs=(ANY,) * len(out_shape),
        scratch_shapes=keep * 4
        + [dma((2, 4, experts)), dma((2, 4, experts)), dma((3, 2)), dma((9,))],
        compiler_params=pltpu.CompilerParams(
            collective_id=1, has_side_effects=True, vmem_limit_bytes=24 << 20
        ),
    )(*pieces(out_terms), *pieces(in_terms), factors)

    def joined(main, rest):
        return jnp.concatenate(
            [main.reshape(experts * TILE, half), rest.reshape(experts, half)], axis=0
        )

    return joined(outs[0], outs[1]), joined(outs[2], outs[3]), outs[4]


def on_device(tokens, routes, gates, cotangent, placement, swap_flag, w_gate, w_up, w_down):
    experts = lax.axis_size("expert")
    myself = lax.axis_index("expert")
    places = jnp.arange(experts, dtype=jnp.int32)
    partner = (places + experts // 2) % experts
    source = jnp.where(swap_flag == 1, partner, places)
    my_flag = jnp.sum(jnp.where(places == myself, swap_flag, 0)) == 1
    held = jnp.sum(jnp.where(source[:, None] == places[None, :], placement[None, :], 0), axis=1)
    tok_count, top_count = routes.shape
    slots_all = experts * CAP
    pair_owner = routes[:, :, None] == held[None, None, :]
    named = jnp.any(pair_owner, axis=1)
    gate_of = jnp.sum(jnp.where(pair_owner, gates[:, :, None].astype(jnp.float32), 0.0), axis=1)
    before = jnp.arange(tok_count)[:, None] > jnp.arange(tok_count)[None, :]
    earlier = jnp.dot(
        before.astype(jnp.bfloat16), named.astype(jnp.bfloat16), preferred_element_type=jnp.float32
    ).astype(jnp.int32)
    rank = jnp.where(named, earlier, CAP)
    column = jnp.arange(slots_all, dtype=jnp.int32)
    in_main = column < experts * TILE
    column_owner = jnp.where(in_main, column // TILE, column - experts * TILE)
    column_slot = jnp.where(in_main, column % TILE, TILE)
    spread = (places[:, None] == column_owner[None, :]).astype(jnp.bfloat16)
    column_rank = jnp.dot(rank.astype(jnp.bfloat16), spread, preferred_element_type=jnp.float32)
    match = column_rank == column_slot[None, :].astype(jnp.float32)
    select = match.astype(jnp.bfloat16)
    column_gate = jnp.dot(gate_of.astype(jnp.bfloat16), spread, preferred_element_type=jnp.float32)
    weighted = jnp.where(match, column_gate, 0.0).astype(jnp.bfloat16)
    contract = (((0,), (0,)), ((), ()))
    inner = (((1,), (1,)), ((), ()))
    outgoing = lax.dot_general(select, tokens, contract, preferred_element_type=jnp.float32).astype(
        jnp.bfloat16
    )
    d_outgoing = lax.dot_general(
        weighted, cotangent, contract, preferred_element_type=jnp.float32
    ).astype(jnp.bfloat16)
    flag = jnp.full((TILE, w_gate.shape[2]), my_flag, jnp.float32)
    expert_in, in_slice, d_out, d_slice, full = gathered(
        outgoing, d_outgoing, (w_gate[0], w_up[0], w_down[0]), flag
    )
    gate_full, up_full, down_full = full
    pre_gate = jnp.dot(expert_in, gate_full, preferred_element_type=jnp.float32)
    pre_up = jnp.dot(expert_in, up_full, preferred_element_type=jnp.float32)
    sig = jax.nn.sigmoid(pre_gate)
    hidden = (pre_gate * sig * pre_up).astype(jnp.bfloat16)
    out_terms = lax.dot_general(hidden, down_full, inner, preferred_element_type=jnp.float32)
    d_hidden = jnp.dot(d_out, down_full, preferred_element_type=jnp.float32)
    d_pre_gate = (d_hidden * pre_up * sig * (1.0 + pre_gate * (1.0 - sig))).astype(jnp.bfloat16)
    d_pre_up = (d_hidden * pre_gate * sig).astype(jnp.bfloat16)
    in_terms = lax.dot_general(d_pre_gate, gate_full, inner, preferred_element_type=jnp.float32)
    in_terms = in_terms + lax.dot_general(
        d_pre_up, up_full, inner, preferred_element_type=jnp.float32
    )
    returned, back_rows, factors = given_back(
        out_terms.astype(jnp.bfloat16),
        in_terms.astype(jnp.bfloat16),
        jnp.concatenate([d_pre_gate, d_pre_up, hidden], axis=1),
    )
    layer_out = jnp.dot(weighted, returned, preferred_element_type=jnp.float32).astype(jnp.bfloat16)
    scores = lax.dot_general(cotangent, returned, inner, preferred_element_type=jnp.float32)
    owner_score = lax.dot_general(
        jnp.where(match, scores, 0.0),
        spread.astype(jnp.float32),
        inner,
        precision=lax.Precision.HIGHEST,
        preferred_element_type=jnp.float32,
    )
    gate_part = jnp.sum(jnp.where(pair_owner, owner_score[:, None, :], 0.0), axis=2)
    gate_grad = lax.psum(gate_part, "tensor")
    input_grad = jnp.dot(select, back_rows, preferred_element_type=jnp.float32).astype(jnp.bfloat16)
    units = hidden.shape[1]
    rows = factors.shape[0] * factors.shape[1]
    factors = factors.reshape(rows, 3 * units)
    in_slice, d_slice = in_slice.reshape(rows, -1), d_slice.reshape(rows, -1)

    def weight_grad(left, which):
        return lax.dot_general(
            left,
            factors[:, which * units : (which + 1) * units],
            contract,
            preferred_element_type=jnp.float32,
        ).astype(jnp.bfloat16)[None]

    return (
        layer_out,
        input_grad,
        gate_grad,
        weight_grad(in_slice, 0),
        weight_grad(in_slice, 1),
        weight_grad(d_slice, 2),
    )


def solution(mesh):
    placed = (
        P(("expert", "dp"), "tensor"),
        P(("expert", "dp"), None),
        P(("expert", "dp"), None),
        P(("expert", "dp"), "tensor"),
        P(),
        P(),
        P("expert", "dp", "tensor"),
        P("expert", "dp", "tensor"),
        P("expert", "dp", "tensor"),
    )
    return jax.shard_map(
        on_device,
        mesh=mesh,
        in_specs=placed,
        out_specs=(
            P(("expert", "dp"), "tensor"),
            P(("expert", "dp"), "tensor"),
            P(("expert", "dp"), None),
            P("expert", "dp", "tensor"),
            P("expert", "dp", "tensor"),
            P("expert", "dp", "tensor"),
        ),
        check_vma=False,
    )
```

```python
import functools

import jax
import jax.numpy as jnp
from jax import lax
from jax.experimental import pallas as pl
from jax.experimental.pallas import tpu as pltpu
from jax.sharding import PartitionSpec as P

CAP = 9
TILE = 8
LANES = 128
PARTS = 2
MESH = pl.DeviceIdType.MESH
ANY = pl.BlockSpec(memory_space=pl.ANY)
WHOLE = pl.BlockSpec(memory_space=pltpu.VMEM)
CONTRACT = (((0,), (0,)), ((), ()))
INNER = (((1,), (1,)), ((), ()))
PLAIN = (((1,), (0,)), ((), ()))


def dot(left, right, dims=PLAIN):
    return lax.dot_general(left, right, dims, preferred_element_type=jnp.float32)


def remote(src, dst, sent, got, where):
    return pltpu.make_async_remote_copy(
        src_ref=src,
        dst_ref=dst,
        send_sem=sent,
        recv_sem=got,
        device_id=where,
        device_id_type=MESH,
    )


def loop(start, stop, body):
    def step(index, carry):
        body(index)
        return carry

    lax.fori_loop(start, stop, step, 0)


def layer_kernel(
    experts, replicas, halves,
    tokens, cotangent, select, weighted, wg, wu, wd, flag,
    layer_out, input_grad, scores, grad_g, grad_u, grad_d,
    x_pack, g_pack, xh, gh, x_rest, g_rest, x_slice, g_slice, x_extra, g_extra,
    arriving, wgf, wuf, wdf, pre, facs, packed, own_o, far_o, got_o, own_i, far_i, got_i,
    ret_o, ret_i, ret_rest,
    a2a_sems, row_sems, slice_sems, weight_sems, tensor_sems, back_sems, factor_sems, local_sems,
):
    me, dp, tensor = lax.axis_index("expert"), lax.axis_index("dp"), lax.axis_index("tensor")
    depth, units = wg.shape
    count = experts * TILE
    all_rows = experts * CAP
    cells = depth // LANES
    block = depth + LANES
    piece = depth // PARTS
    own, full = (wg, wu, wd), (wgf, wuf, wdf)
    sibling = {"dp": dp + 1 - 2 * (dp % 2)}
    across_dp = (dp + 2) % replicas
    across = {"dp": across_dp}
    far = 1 - tensor
    opposite = {"tensor": far}
    bf16, f32 = jnp.bfloat16, jnp.float32

    barrier = pltpu.get_barrier_semaphore()
    group = replicas * halves

    def along(step):
        pl.semaphore_signal(
            barrier, inc=1, device_id={"expert": (me + step) % experts}, device_id_type=MESH
        )

    def inside(step):
        other = (dp * halves + tensor + step) % group
        pl.semaphore_signal(
            barrier,
            inc=1,
            device_id={"dp": other // halves, "tensor": other % halves},
            device_id_type=MESH,
        )

    loop(1, experts, along)
    loop(1, group, inside)

    wide = cells * experts
    line = lax.broadcasted_iota(jnp.int32, (wide, count), 0)
    place = lax.broadcasted_iota(jnp.int32, (wide, count), 1)
    unpacking = ((line % experts) * TILE + line // experts == place).astype(f32).astype(bf16)
    line = lax.broadcasted_iota(jnp.int32, (count, wide), 1)
    place = lax.broadcasted_iota(jnp.int32, (count, wide), 0)
    packing = ((line % experts) * TILE + line // experts == place).astype(f32).astype(bf16)

    def slab(which):
        return pl.ds(pl.multiple_of(which * TILE, TILE), TILE)

    def put(values, index, target):
        target[:, index * block : index * block + depth] = values[:count]
        for cell in range(cells):
            packed[cell * experts : (cell + 1) * experts, index * LANES : (index + 1) * LANES] = (
                values[count:, cell * LANES : (cell + 1) * LANES]
            )

    def put_extra(target):
        extra = dot(packing, packed[...]).astype(bf16)
        for index in range(2):
            target[:, index * block + depth : (index + 1) * block] = extra[
                :, index * LANES : (index + 1) * LANES
            ]

    def rest_of(extra, target, index, first=0):
        rows = dot(unpacking, extra).astype(bf16)
        for cell in range(cells):
            column = index * depth + cell * LANES
            target[first : first + experts, column : column + LANES] = rows[
                cell * experts : (cell + 1) * experts
            ]

    def rows(part):
        return pl.ds(part * piece, piece)

    def region(which, part):
        return pl.ds(pl.multiple_of(which * depth + part * piece, 64), piece)

    def swap(matrix, part):
        sems = weight_sems.at[0, matrix, part]
        return remote(
            own[matrix].at[rows(part)], arriving.at[matrix, rows(part)],
            sems.at[0], sems.at[1], {"expert": (me + experts // 2) % experts},
        )

    def stay(matrix):
        mine = pl.ds(pl.multiple_of(dp * depth, 64), depth)
        return pltpu.make_async_copy(own[matrix], full[matrix].at[mine], local_sems.at[2 + matrix])

    def spread(matrix, part, kind):
        at = region(across_dp if kind == 2 else dp, part)
        sems = weight_sems.at[1 + kind, matrix, part]
        return remote(
            full[matrix].at[at], full[matrix].at[at], sems.at[0], sems.at[1],
            across if kind == 1 else sibling,
        )

    sides = (
        (tokens, select, x_pack, xh, x_slice, x_extra),
        (cotangent, weighted, g_pack, gh, g_slice, g_extra),
    )

    def out_slab(index, step):
        pack, to = sides[index][2:4]
        peer = (me + step) % experts
        return remote(
            pack.at[slab(peer)], to.at[tensor, slab(me)],
            a2a_sems.at[index, 0, step], a2a_sems.at[index, 1, step], {"expert": peer},
        )

    def own_slab(index):
        pack, to = sides[index][2:4]
        return pltpu.make_async_copy(
            pack.at[slab(me)], to.at[tensor, slab(me)], local_sems.at[index]
        )

    for matrix in range(3):
        stay(matrix).start()
    for index in range(2):
        data, picks, pack = sides[index][:3]
        for part in range(2):
            values = dot(picks[...], data[:, part * depth : (part + 1) * depth], CONTRACT)
            put(values.astype(bf16), part, pack)
        put_extra(pack)
        if index == 0:
            pl.semaphore_wait(barrier, experts - 1 + group - 1)
        own_slab(index).start()
        loop(1, experts, lambda step, index=index: out_slab(index, step).start())
    order = [(matrix, part) for matrix in range(3) for part in range(PARTS)]
    for matrix, part in order:
        swap(matrix, part).start()

    def row_copy(index):
        to = sides[index][3]
        return remote(
            to.at[tensor], to.at[tensor], row_sems.at[index, 0], row_sems.at[index, 1], opposite
        )

    def slice_refs(index, part):
        to, main, extra = sides[index][3:]
        return (
            (to.at[tensor, :, part * block : part * block + depth],
             main.at[pl.ds(pl.multiple_of(dp * all_rows, 32), count)]),
            (to.at[tensor, :, part * block + depth : (part + 1) * block],
             extra.at[pl.ds(pl.multiple_of(dp * count, 32), count)]),
        )

    def slice_copies(index, part, stays):
        where = {"dp": tensor * 2 + part, "tensor": tensor if stays else far}
        sent = slice_sems.at[index, 0, 2 * part + stays]
        got = slice_sems.at[index, 1, dp]
        return [
            remote(src, dst, sent.at[number], got.at[number], where)
            for number, (src, dst) in enumerate(slice_refs(index, part))
        ]

    def slice_here(index, part):
        got = slice_sems.at[index, 1, dp]
        return [
            pltpu.make_async_copy(src, dst, got.at[number])
            for number, (src, dst) in enumerate(slice_refs(index, part))
        ]

    for index in range(2):
        own_slab(index).wait()
        loop(1, experts, lambda step, index=index: out_slab(index, step).wait_recv())
        row_copy(index).start()
        for part in range(2):
            for copy in slice_copies(index, part, 0):
                copy.start()

            @pl.when(dp == tensor * 2 + part)
            def _(index=index, part=part):
                for copy in slice_here(index, part):
                    copy.start()

            @pl.when(dp != tensor * 2 + part)
            def _(index=index, part=part):
                for copy in slice_copies(index, part, 1):
                    copy.start()

    def forward(matrix, part):
        spread(matrix, part, 1).wait_recv()
        spread(matrix, part, 2).start()

    def complete(matrix):
        for part in range(PARTS):
            spread(matrix, part, 0).wait_recv()
            spread(matrix, part, 2).wait_recv()

    def unpack_rows(index):
        row_copy(index).wait_recv()
        to, rest = sides[index][3], (x_rest, g_rest)[index]
        for number in range(2 * halves):
            at = (number % 2) * block + depth
            rest_of(to[number // 2, :, at : at + LANES], rest, number)

    def project(index, matrix):
        to, rest = sides[index][3], (x_rest, g_rest)[index]
        for number in range(2 * halves):
            at = (number % 2) * block
            left = jnp.concatenate(
                [
                    to[number // 2, :, at : at + depth],
                    rest[:, number * depth : (number + 1) * depth],
                ],
                axis=0,
            )
            term = dot(left, full[matrix][number * depth : (number + 1) * depth, :])
            pre[matrix] = term if number == 0 else pre[matrix] + term

    taken = flag[0:1, :]
    for number, (matrix, part) in enumerate(order):
        if part == 0:
            stay(matrix).wait()
        swap(matrix, part).wait_recv()

        def choose(step, matrix=matrix, part=part):
            lines = pl.ds(pl.multiple_of(part * piece + step * 64, 64), 64)
            at = pl.ds(pl.multiple_of(dp * depth + part * piece + step * 64, 64), 64)
            fresh = arriving[matrix, lines, :].astype(f32)
            former = full[matrix][at, :].astype(f32)
            full[matrix][at, :] = (fresh * taken + former * (1.0 - taken)).astype(bf16)

        loop(0, piece // 64, choose)
        spread(matrix, part, 1).start()
        spread(matrix, part, 0).start()
        if number > 0:
            forward(*order[number - 1])
        if (matrix, part) == (1, 0):
            unpack_rows(0)
        if (matrix, part) == (1, PARTS - 1):
            complete(0)
            project(0, 0)
        if (matrix, part) == (2, 0):
            unpack_rows(1)
        if (matrix, part) == (2, PARTS - 1):
            complete(1)
            project(0, 1)
    forward(*order[-1])

    strip = 32

    def factor_rows(step):
        return pl.ds(pl.multiple_of(dp * all_rows + step * strip, 32), strip)

    def hide(step):
        lines = pl.ds(pl.multiple_of(step * strip, strip), strip)
        gate, up = pre[0, lines, :], pre[1, lines, :]
        facs[factor_rows(step), 2 * units :] = (gate * jax.nn.sigmoid(gate) * up).astype(bf16)

    loop(0, all_rows // strip, hide)
    complete(2)

    def to_terms(lefts, matrices, which, target):
        for part in range(2):
            at = pl.ds(pl.multiple_of((which * 2 + part) * depth, 64), depth)
            terms = None
            for left, matrix in zip(lefts, matrices):
                term = dot(left, full[matrix][at, :], INNER)
                terms = term if terms is None else terms + term
            put(terms.astype(bf16), part, target)
        put_extra(target)

    backs = ((own_o, far_o, got_o, ret_o), (own_i, far_i, got_i, ret_i))

    couples = experts // 2

    def couple(step):
        return (me // 2 + step) % couples

    def both(step):
        return pl.ds(pl.multiple_of(couple(step) * 2 * TILE, 2 * TILE), 2 * TILE)

    def half_over(index, step):
        terms, got = backs[index][1:3]
        return remote(
            terms.at[both(step)], got.at[both(step)],
            tensor_sems.at[index, 0, step], tensor_sems.at[index, 1, step], opposite,
        )

    def back(index, step, member):
        terms, to = backs[index][0], backs[index][3]
        peer = couple(step) * 2 + member
        return remote(
            terms.at[slab(peer)], to.at[slab(me)],
            back_sems.at[index, 0, 2 * step + member], back_sems.at[index, 1, 2 * step + me % 2],
            {"expert": peer},
        )

    def back_come(index, step, member):
        terms, to = backs[index][0], backs[index][3]
        peer = couple(step) * 2 + member
        return remote(
            terms.at[slab(peer)], to.at[slab(me)],
            back_sems.at[index, 0, 2 * step + member], back_sems.at[index, 1, 2 * step + member],
            {"expert": peer},
        )

    def back_here(index):
        terms, to = backs[index][0], backs[index][3]
        return pltpu.make_async_copy(terms.at[slab(me)], to.at[slab(me)], local_sems.at[5 + index])

    mine = pl.ds(pl.multiple_of(dp * all_rows, 32), all_rows)
    hidden = facs[mine, 2 * units :]
    to_terms([hidden], [2], far, far_o)
    loop(0, couples, lambda step: half_over(0, step).start())
    to_terms([hidden], [2], tensor, own_o)

    project(1, 2)

    def differentiate(step):
        lines = pl.ds(pl.multiple_of(step * strip, strip), strip)
        gate, up, d_hidden = pre[0, lines, :], pre[1, lines, :], pre[2, lines, :]
        sig = jax.nn.sigmoid(gate)
        at = factor_rows(step)
        facs[at, :units] = (d_hidden * up * sig * (1.0 + gate * (1.0 - sig))).astype(bf16)
        facs[at, units : 2 * units] = (d_hidden * gate * sig).astype(bf16)

    loop(0, all_rows // strip, differentiate)
    d_gate, d_up = facs[mine, :units], facs[mine, units : 2 * units]
    to_terms([d_gate, d_up], [0, 1], far, far_i)
    loop(0, couples, lambda step: half_over(1, step).start())

    def factor(kind):
        which = across_dp if kind == 2 else dp
        at = pl.ds(pl.multiple_of(which * all_rows, 32), all_rows)
        return remote(
            facs.at[at], facs.at[at], factor_sems.at[kind, 0], factor_sems.at[kind, 1],
            across if kind == 1 else sibling,
        )

    factor(1).start()
    factor(0).start()
    to_terms([d_gate, d_up], [0, 1], tensor, own_i)

    def add(index, step):
        half_over(index, step).wait_recv()
        terms, got = backs[index][0], backs[index][2]
        at = both(step)
        terms[at, :] = (terms[at, :].astype(f32) + got[at, :].astype(f32)).astype(bf16)

    def pass_on(index, step):
        add(index, step)
        for member in range(2):
            back(index, step, member).start()

    for index in range(2):
        loop(1, couples, lambda step, index=index: pass_on(index, step))
        add(index, 0)
        back(index, 0, 1 - me % 2).start()
        back_here(index).start()

    factor(1).wait_recv()
    factor(2).start()

    def returned(index):
        back_here(index).wait()
        back_come(index, 0, 1 - me % 2).wait_recv()

        def come(step):
            for member in range(2):
                back_come(index, step, member).wait_recv()

        loop(1, couples, come)
        to = backs[index][3]
        for part in range(2):
            at = part * block + depth
            rest_of(to[:, at : at + LANES], ret_rest, part)
        return [
            jnp.concatenate(
                [
                    to[:, part * block : part * block + depth],
                    ret_rest[:, part * depth : (part + 1) * depth],
                ],
                axis=0,
            )
            for part in range(2)
        ]

    def slices_landed(index):
        to, main, extra = sides[index][3:]

        def landed(source):
            got = slice_sems.at[index, 1, source]
            at = pl.ds(pl.multiple_of(source * all_rows, 32), count)
            pltpu.make_async_copy(main.at[at], main.at[at], got.at[0]).wait()
            at = pl.ds(pl.multiple_of(source * count, 32), count)
            pltpu.make_async_copy(extra.at[at], extra.at[at], got.at[1]).wait()

        loop(0, replicas, landed)
        for source in range(replicas):
            rest_of(
                extra[source * count : (source + 1) * count, :],
                main,
                0,
                source * all_rows + count,
            )

    for index in range(2):
        slices_landed(index)
    for part, values in enumerate(returned(0)):
        at = slice(part * depth, (part + 1) * depth)
        layer_out[:, at] = dot(weighted[...], values).astype(bf16)
        term = dot(cotangent[:, at], values, INNER)
        scores[...] = term if part == 0 else scores[...] + term

    factor(0).wait_recv()
    factor(2).wait_recv()
    cuts = (0, 512, depth) if depth > 512 else (0, depth)
    for index, (left, grad) in enumerate(((x_slice, grad_g), (x_slice, grad_u), (g_slice, grad_d))):
        right = facs[:, index * units : (index + 1) * units]
        for low, high in zip(cuts, cuts[1:]):
            grad[low:high, :] = dot(left[:, low:high], right, CONTRACT).astype(bf16)

    for part, values in enumerate(returned(1)):
        at = slice(part * depth, (part + 1) * depth)
        input_grad[:, at] = dot(select[...], values).astype(bf16)

    for matrix, part in order:
        swap(matrix, part).wait_send()
        for kind in range(3):
            spread(matrix, part, kind).wait_send()
    for kind in range(3):
        factor(kind).wait_send()
    for index in range(2):
        loop(1, experts, lambda step, index=index: out_slab(index, step).wait_send())
        back(index, 0, 1 - me % 2).wait_send()

        def gone(step, index=index):
            for member in range(2):
                back(index, step, member).wait_send()

        loop(1, couples, gone)
        loop(0, couples, lambda step, index=index: half_over(index, step).wait_send())
        row_copy(index).wait_send()
        for part in range(2):
            for copy in slice_copies(index, part, 0):
                copy.wait_send()

            @pl.when(dp != tensor * 2 + part)
            def _(index=index, part=part):
                for copy in slice_copies(index, part, 1):
                    copy.wait_send()


def layer(tokens, cotangent, select, weighted, weights, flag):
    experts, replicas, halves = (lax.axis_size(a) for a in ("expert", "dp", "tensor"))
    depth, units = weights[0].shape
    count, all_rows = experts * TILE, experts * CAP
    block, cells = depth + LANES, depth // LANES
    own_rows, half = tokens.shape

    def like(*shape, dtype=jnp.bfloat16):
        return jax.ShapeDtypeStruct(shape, dtype)

    def keep(*shape, dtype=jnp.bfloat16):
        return pltpu.VMEM(shape, dtype)

    out_shape = (
        like(own_rows, half),
        like(own_rows, half),
        like(own_rows, all_rows, dtype=jnp.float32),
    ) + (like(depth, units),) * 3
    dma = pltpu.SemaphoreType.DMA
    return pl.pallas_call(
        functools.partial(layer_kernel, experts, replicas, halves),
        name="layer",
        out_shape=out_shape,
        in_specs=[WHOLE] * 4 + [ANY] * 3 + [WHOLE],
        out_specs=(WHOLE,) * len(out_shape),
        scratch_shapes=[keep(count, 2 * block)] * 2
        + [keep(halves, count, 2 * block)] * 2
        + [keep(experts, halves * half)] * 2
        + [keep(replicas * all_rows, depth)] * 2
        + [keep(replicas * count, LANES)] * 2
        + [keep(3, depth, units)]
        + [keep(replicas * depth, units)] * 3
        + [
            keep(3, all_rows, units, dtype=jnp.float32),
            keep(replicas * all_rows, 3 * units),
            keep(cells * experts, 2 * LANES),
        ]
        + [keep(count, 2 * block)] * 8
        + [keep(experts, half)]
        + [
            dma((2, 2, experts)),
            dma((2, 2)),
            dma((2, 2, 4, 2)),
            dma((4, 3, PARTS, 2)),
            dma((2, 2, experts)),
            dma((2, 2, experts)),
            dma((3, 2)),
            dma((7,)),
        ],
        compiler_params=pltpu.CompilerParams(
            collective_id=0, has_side_effects=True, vmem_limit_bytes=60 << 20
        ),
    )(tokens, cotangent, select, weighted, *weights, flag)


def on_device(tokens, routes, gates, cotangent, placement, swap_flag, w_gate, w_up, w_down):
    experts = lax.axis_size("expert")
    myself = lax.axis_index("expert")
    places = jnp.arange(experts, dtype=jnp.int32)
    partner = (places + experts // 2) % experts
    source = jnp.where(swap_flag == 1, partner, places)
    my_flag = jnp.sum(jnp.where(places == myself, swap_flag, 0)) == 1
    held = jnp.sum(jnp.where(source[:, None] == places[None, :], placement[None, :], 0), axis=1)
    tok_count, top_count = routes.shape
    slots_all = experts * CAP
    pair_owner = routes[:, :, None] == held[None, None, :]
    named = jnp.any(pair_owner, axis=1)
    gate_of = jnp.sum(jnp.where(pair_owner, gates[:, :, None].astype(jnp.float32), 0.0), axis=1)
    before = jnp.arange(tok_count)[:, None] > jnp.arange(tok_count)[None, :]
    earlier = jnp.dot(
        before.astype(jnp.bfloat16), named.astype(jnp.bfloat16), preferred_element_type=jnp.float32
    ).astype(jnp.int32)
    rank = jnp.where(named, earlier, CAP)
    column = jnp.arange(slots_all, dtype=jnp.int32)
    in_main = column < experts * TILE
    column_owner = jnp.where(in_main, column // TILE, column - experts * TILE)
    column_slot = jnp.where(in_main, column % TILE, TILE)
    spread = (places[:, None] == column_owner[None, :]).astype(jnp.bfloat16)
    column_rank = jnp.dot(rank.astype(jnp.bfloat16), spread, preferred_element_type=jnp.float32)
    match = column_rank == column_slot[None, :].astype(jnp.float32)
    select = match.astype(jnp.bfloat16)
    column_gate = jnp.dot(gate_of.astype(jnp.bfloat16), spread, preferred_element_type=jnp.float32)
    weighted = jnp.where(match, column_gate, 0.0).astype(jnp.bfloat16)
    flag = jnp.full((TILE, w_gate.shape[2]), my_flag, jnp.float32)
    layer_out, input_grad, scores, *grads = layer(
        tokens, cotangent, select, weighted, (w_gate[0], w_up[0], w_down[0]), flag
    )
    owner_score = lax.dot_general(
        jnp.where(match, scores, 0.0),
        spread.astype(jnp.float32),
        INNER,
        precision=lax.Precision.HIGHEST,
        preferred_element_type=jnp.float32,
    )
    gate_part = jnp.sum(jnp.where(pair_owner, owner_score[:, None, :], 0.0), axis=2)
    gate_grad = lax.psum(gate_part, "tensor")
    return (layer_out, input_grad, gate_grad, *(grad[None] for grad in grads))


def solution(mesh):
    placed = (
        P(("expert", "dp"), "tensor"),
        P(("expert", "dp"), None),
        P(("expert", "dp"), None),
        P(("expert", "dp"), "tensor"),
        P(),
        P(),
        P("expert", "dp", "tensor"),
        P("expert", "dp", "tensor"),
        P("expert", "dp", "tensor"),
    )
    return jax.shard_map(
        on_device,
        mesh=mesh,
        in_specs=placed,
        out_specs=(
            P(("expert", "dp"), "tensor"),
            P(("expert", "dp"), "tensor"),
            P(("expert", "dp"), None),
            P("expert", "dp", "tensor"),
            P("expert", "dp", "tensor"),
            P("expert", "dp", "tensor"),
        ),
        check_vma=False,
    )
```

```python
import functools

import jax
import jax.numpy as jnp
from jax import lax
from jax.experimental import pallas as pl
from jax.experimental.pallas import tpu as pltpu
from jax.sharding import PartitionSpec as P

CAP = 9
TILE = 8
LANES = 128
PARTS = 7
MESH = pl.DeviceIdType.MESH
ANY = pl.BlockSpec(memory_space=pl.ANY)
WHOLE = pl.BlockSpec(memory_space=pltpu.VMEM)
CONTRACT = (((0,), (0,)), ((), ()))
INNER = (((1,), (1,)), ((), ()))
PLAIN = (((1,), (0,)), ((), ()))


def dot(left, right, dims=PLAIN):
    return lax.dot_general(left, right, dims, preferred_element_type=jnp.float32)


def remote(src, dst, sent, got, where):
    return pltpu.make_async_remote_copy(
        src_ref=src,
        dst_ref=dst,
        send_sem=sent,
        recv_sem=got,
        device_id=where,
        device_id_type=MESH,
    )


def loop(start, stop, body):
    def step(index, carry):
        body(index)
        return carry

    lax.fori_loop(start, stop, step, 0)


def layer_kernel(
    experts, replicas, halves,
    tokens, cotangent, select, weighted, wg, wu, wd, flag,
    layer_out, input_grad, owner_scores, grad_g, grad_u, grad_d,
    x_pack, g_pack, xh, gh, x_rest, g_rest, x_slice, g_slice, x_extra, g_extra,
    arriving, wgf, wuf, wdf, pre, facs, packed, packed_far, packed_own, own_o, far_o, got_o, own_i, far_i, got_i,
    ret_o, ret_i, ret_rest, part_scores, other_scores,
    a2a_sems, row_sems, slice_sems, weight_sems, tensor_sems, piece_sems, back_sems, factor_sems, local_sems,
):
    me, dp, tensor = lax.axis_index("expert"), lax.axis_index("dp"), lax.axis_index("tensor")
    depth, units = wg.shape
    count = experts * TILE
    all_rows = experts * CAP
    cells = depth // LANES
    block = depth + LANES
    piece = depth // PARTS
    own, full = (wg, wu, wd), (wgf, wuf, wdf)
    sibling = {"dp": dp + 1 - 2 * (dp % 2)}
    across_dp = (dp + 2) % replicas
    across = {"dp": across_dp}
    far = 1 - tensor
    opposite = {"tensor": far}
    bf16, f32 = jnp.bfloat16, jnp.float32

    barrier = pltpu.get_barrier_semaphore()
    group = replicas * halves

    def along(step):
        pl.semaphore_signal(
            barrier, inc=1, device_id={"expert": (me + step) % experts}, device_id_type=MESH
        )

    def inside(step):
        other = (dp * halves + tensor + step) % group
        pl.semaphore_signal(
            barrier,
            inc=1,
            device_id={"dp": other // halves, "tensor": other % halves},
            device_id_type=MESH,
        )

    loop(1, experts, along)
    loop(1, group, inside)

    wide = cells * experts
    line = lax.broadcasted_iota(jnp.int32, (wide, count), 0)
    place = lax.broadcasted_iota(jnp.int32, (wide, count), 1)
    unpacking = ((line % experts) * TILE + line // experts == place).astype(f32).astype(bf16)
    line = lax.broadcasted_iota(jnp.int32, (count, wide), 1)
    place = lax.broadcasted_iota(jnp.int32, (count, wide), 0)
    packing = ((line % experts) * TILE + line // experts == place).astype(f32).astype(bf16)

    def slab(which):
        return pl.ds(pl.multiple_of(which * TILE, TILE), TILE)

    def put(values, index, target):
        target[:, index * block : index * block + depth] = values[:count]
        for cell in range(cells):
            packed[cell * experts : (cell + 1) * experts, index * LANES : (index + 1) * LANES] = (
                values[count:, cell * LANES : (cell + 1) * LANES]
            )

    def put_extra(target, packed=packed):
        extra = dot(packing, packed[...]).astype(bf16)
        for index in range(2):
            target[:, index * block + depth : (index + 1) * block] = extra[
                :, index * LANES : (index + 1) * LANES
            ]

    def rest_of(extra, target, index, first=0):
        rows = dot(unpacking, extra).astype(bf16)
        for cell in range(cells):
            column = index * depth + cell * LANES
            target[first : first + experts, column : column + LANES] = rows[
                cell * experts : (cell + 1) * experts
            ]

    def rows(part):
        return pl.ds(pl.multiple_of(part * piece, 64), piece)

    def region(which, part):
        return pl.ds(pl.multiple_of(which * depth + part * piece, 64), piece)

    def swap(matrix, part):
        sems = weight_sems.at[0, matrix, part]
        return remote(
            own[matrix].at[rows(part)], arriving.at[matrix, rows(part)],
            sems.at[0], sems.at[1], {"expert": (me + experts // 2) % experts},
        )

    def stay(matrix):
        mine = pl.ds(pl.multiple_of(dp * depth, 64), depth)
        return pltpu.make_async_copy(own[matrix], full[matrix].at[mine], local_sems.at[2 + matrix])

    def spread(matrix, part, kind):
        at = region(across_dp if kind == 2 else dp, part)
        sems = weight_sems.at[1 + kind, matrix, part]
        return remote(
            full[matrix].at[at], full[matrix].at[at], sems.at[0], sems.at[1],
            across if kind == 1 else sibling,
        )

    sides = (
        (tokens, select, x_pack, xh, x_slice, x_extra),
        (cotangent, weighted, g_pack, gh, g_slice, g_extra),
    )

    def out_slab(index, step):
        pack, to = sides[index][2:4]
        peer = (me + step) % experts
        return remote(
            pack.at[slab(peer)], to.at[tensor, slab(me)],
            a2a_sems.at[index, 0, step], a2a_sems.at[index, 1, step], {"expert": peer},
        )

    def own_slab(index):
        pack, to = sides[index][2:4]
        return pltpu.make_async_copy(
            pack.at[slab(me)], to.at[tensor, slab(me)], local_sems.at[index]
        )

    for matrix in range(3):
        stay(matrix).start()
    for index in range(2):
        data, picks, pack = sides[index][:3]
        for part in range(2):
            values = dot(picks[...], data[:, part * depth : (part + 1) * depth], CONTRACT)
            put(values.astype(bf16), part, pack)
        put_extra(pack)
        if index == 0:
            pl.semaphore_wait(barrier, experts - 1 + group - 1)
        own_slab(index).start()
        loop(1, experts, lambda step, index=index: out_slab(index, step).start())
    for matrix in range(3):
        loop(0, PARTS, lambda part, matrix=matrix: swap(matrix, part).start())

    def row_copy(index):
        to = sides[index][3]
        return remote(
            to.at[tensor], to.at[tensor], row_sems.at[index, 0], row_sems.at[index, 1], opposite
        )

    def slice_refs(index, part):
        to, main, extra = sides[index][3:]
        return (
            (to.at[tensor, :, part * block : part * block + depth],
             main.at[pl.ds(pl.multiple_of(dp * all_rows, 32), count)]),
            (to.at[tensor, :, part * block + depth : (part + 1) * block],
             extra.at[pl.ds(pl.multiple_of(dp * count, 32), count)]),
        )

    def slice_copies(index, part, stays):
        where = {"dp": tensor * 2 + part, "tensor": tensor if stays else far}
        sent = slice_sems.at[index, 0, 2 * part + stays]
        got = slice_sems.at[index, 1, dp]
        return [
            remote(src, dst, sent.at[number], got.at[number], where)
            for number, (src, dst) in enumerate(slice_refs(index, part))
        ]

    def slice_here(index, part):
        got = slice_sems.at[index, 1, dp]
        return [
            pltpu.make_async_copy(src, dst, got.at[number])
            for number, (src, dst) in enumerate(slice_refs(index, part))
        ]

    for index in range(2):
        own_slab(index).wait()
        loop(1, experts, lambda step, index=index: out_slab(index, step).wait_recv())
        row_copy(index).start()
        for part in range(2):
            for copy in slice_copies(index, part, 0):
                copy.start()

            @pl.when(dp == tensor * 2 + part)
            def _(index=index, part=part):
                for copy in slice_here(index, part):
                    copy.start()

            @pl.when(dp != tensor * 2 + part)
            def _(index=index, part=part):
                for copy in slice_copies(index, part, 1):
                    copy.start()

    def forward(matrix, part):
        spread(matrix, part, 1).wait_recv()
        spread(matrix, part, 2).start()

    def complete(matrix):
        def here(part):
            spread(matrix, part, 0).wait_recv()
            spread(matrix, part, 2).wait_recv()

        loop(0, PARTS, here)

    def unpack_rows(index):
        row_copy(index).wait_recv()
        to, rest = sides[index][3], (x_rest, g_rest)[index]
        for number in range(2 * halves):
            at = (number % 2) * block + depth
            rest_of(to[number // 2, :, at : at + LANES], rest, number)

    def project(index, matrix):
        to, rest = sides[index][3], (x_rest, g_rest)[index]
        for number in range(2 * halves):
            at = (number % 2) * block
            left = jnp.concatenate(
                [
                    to[number // 2, :, at : at + depth],
                    rest[:, number * depth : (number + 1) * depth],
                ],
                axis=0,
            )
            term = dot(left, full[matrix][number * depth : (number + 1) * depth, :])
            pre[matrix] = term if number == 0 else pre[matrix] + term

    strip = 32

    def factor_rows(step):
        return pl.ds(pl.multiple_of(dp * all_rows + step * strip, 32), strip)

    def hide(step):
        lines = pl.ds(pl.multiple_of(step * strip, strip), strip)
        gate, up = pre[0, lines, :], pre[1, lines, :]
        facs[factor_rows(step), 2 * units :] = (gate * jax.nn.sigmoid(gate) * up).astype(bf16)

    def to_terms(lefts, matrices, which, target):
        for part in range(2):
            at = pl.ds(pl.multiple_of((which * 2 + part) * depth, 64), depth)
            terms = None
            for left, matrix in zip(lefts, matrices):
                term = dot(left, full[matrix][at, :], INNER)
                terms = term if terms is None else terms + term
            put(terms.astype(bf16), part, target)
        put_extra(target)

    backs = ((own_o, far_o, got_o, ret_o), (own_i, far_i, got_i, ret_i))

    couples = experts // 2

    def couple(step):
        return (me // 2 + step) % couples

    def both(step):
        return pl.ds(pl.multiple_of(couple(step) * 2 * TILE, 2 * TILE), 2 * TILE)

    def half_over(step):
        return remote(
            far_i.at[both(step)], got_i.at[both(step)],
            tensor_sems.at[0, step], tensor_sems.at[1, step], opposite,
        )

    def back(index, step, member):
        terms, to = backs[index][0], backs[index][3]
        peer = couple(step) * 2 + member
        return remote(
            terms.at[slab(peer)], to.at[slab(me)],
            back_sems.at[index, 0, 2 * step + member], back_sems.at[index, 1, 2 * step + me % 2],
            {"expert": peer},
        )

    def back_come(index, step, member):
        terms, to = backs[index][0], backs[index][3]
        peer = couple(step) * 2 + member
        return remote(
            terms.at[slab(peer)], to.at[slab(me)],
            back_sems.at[index, 0, 2 * step + member], back_sems.at[index, 1, 2 * step + member],
            {"expert": peer},
        )

    def back_here(index):
        terms, to = backs[index][0], backs[index][3]
        return pltpu.make_async_copy(terms.at[slab(me)], to.at[slab(me)], local_sems.at[5 + index])

    def factor(kind, late):
        which = across_dp if kind == 2 else dp
        at = pl.ds(pl.multiple_of(which * all_rows, 32), all_rows)
        cut = slice(0, 2 * units) if late else slice(2 * units, 3 * units)
        sems = factor_sems.at[late, kind]
        return remote(
            facs.at[at, cut], facs.at[at, cut], sems.at[0], sems.at[1],
            across if kind == 1 else sibling,
        )

    def slices_landed(index):
        to, main, extra = sides[index][3:]

        def landed(source):
            got = slice_sems.at[index, 1, source]
            at = pl.ds(pl.multiple_of(source * all_rows, 32), count)
            pltpu.make_async_copy(main.at[at], main.at[at], got.at[0]).wait()
            at = pl.ds(pl.multiple_of(source * count, 32), count)
            pltpu.make_async_copy(extra.at[at], extra.at[at], got.at[1]).wait()

        loop(0, replicas, landed)
        for source in range(replicas):
            rest_of(
                extra[source * count : (source + 1) * count, :],
                main,
                0,
                source * all_rows + count,
            )

    def weight_grad(index):
        left, grad = ((x_slice, grad_g), (x_slice, grad_u), (g_slice, grad_d))[index]
        right = facs[:, index * units : (index + 1) * units]
        cuts = (0, 512, depth) if depth > 512 else (0, depth)
        for low, high in zip(cuts, cuts[1:]):
            grad[low:high, :] = dot(left[:, low:high], right, CONTRACT).astype(bf16)

    mine = pl.ds(pl.multiple_of(dp * all_rows, 32), all_rows)
    taken = flag[0:1, :]

    def take(matrix, part):
        swap(matrix, part).wait_recv()
        for step in range(piece // 64):
            lines = pl.ds(pl.multiple_of(part * piece + step * 64, 64), 64)
            at = pl.ds(pl.multiple_of(dp * depth + part * piece + step * 64, 64), 64)
            fresh = arriving[matrix, lines, :].astype(f32)
            former = full[matrix][at, :].astype(f32)
            full[matrix][at, :] = (fresh * taken + former * (1.0 - taken)).astype(bf16)
        spread(matrix, part, 1).start()
        spread(matrix, part, 0).start()

    def take_and_forward(matrix, part):
        take(matrix, part)
        forward(matrix, part - 1)

    def piece_over(part, side):
        at = side * block + part * piece
        number = 2 * part + side
        return remote(
            far_o.at[:, at : at + piece], got_o.at[:, at : at + piece],
            piece_sems.at[0, number], piece_sems.at[1, number], opposite,
        )

    def use_down(part):
        spread(2, part, 0).wait_recv()
        spread(2, part, 2).wait_recv()
        hidden = facs[mine, 2 * units :]
        low = part * piece
        for which, target, wide_form in ((far, far_o, packed_far), (tensor, own_o, packed_own)):
            for side in range(2):
                at = pl.ds(pl.multiple_of((which * 2 + side) * depth + low, 64), piece)
                values = dot(hidden, full[2][at, :], INNER).astype(bf16)
                target[:, side * block + low : side * block + low + piece] = values[:count]
                for cell in range(piece // LANES):
                    line = (low // LANES + cell) * experts
                    wide_form[line : line + experts, side * LANES : (side + 1) * LANES] = values[
                        count:, cell * LANES : (cell + 1) * LANES
                    ]
            if target is far_o:
                for side in range(2):
                    piece_over(part, side).start()
        total = None
        for number in range(2 * halves):
            at = (number % 2) * block + low
            left = jnp.concatenate(
                [
                    gh[number // 2, :, at : at + piece],
                    g_rest[:, number * depth + low : number * depth + low + piece],
                ],
                axis=0,
            )
            at = number * depth + low
            term = dot(left, full[2][at : at + piece, :])
            total = term if total is None else total + term
        pre[2] = total if part == 0 else pre[2] + total

    for matrix in range(2):
        stay(matrix).wait()
        take(matrix, 0)
        if matrix:
            forward(0, PARTS - 1)
        loop(1, PARTS, lambda part, matrix=matrix: take_and_forward(matrix, part))
    stay(2).wait()
    for part in range(PARTS):
        take(2, part)
        forward(*((1, PARTS - 1) if part == 0 else (2, part - 1)))
        if part == 0:
            unpack_rows(0)
            complete(0)
            project(0, 0)
        if part == 1:
            unpack_rows(1)
        if part == 2:
            complete(1)
            project(0, 1)
            loop(0, all_rows // strip, hide)
            factor(1, 0).start()
            factor(0, 0).start()
        if part == 3:
            slices_landed(1)
        if part == 4:
            slices_landed(0)
        if part == 5:
            factor(1, 0).wait_recv()
            factor(2, 0).start()
        if part >= 2:
            use_down(part - 2)
    forward(2, PARTS - 1)
    use_down(PARTS - 2)
    use_down(PARTS - 1)
    put_extra(far_o, packed_far)
    for side in range(2):
        piece_over(PARTS, side).start()

    def differentiate(step):
        lines = pl.ds(pl.multiple_of(step * strip, strip), strip)
        gate, up, d_hidden = pre[0, lines, :], pre[1, lines, :], pre[2, lines, :]
        sig = jax.nn.sigmoid(gate)
        at = factor_rows(step)
        facs[at, :units] = (d_hidden * up * sig * (1.0 + gate * (1.0 - sig))).astype(bf16)
        facs[at, units : 2 * units] = (d_hidden * gate * sig).astype(bf16)

    loop(0, all_rows // strip, differentiate)
    d_gate, d_up = facs[mine, :units], facs[mine, units : 2 * units]
    to_terms([d_gate, d_up], [0, 1], far, far_i)
    loop(0, couples, lambda step: half_over(step).start())
    factor(1, 1).start()
    factor(0, 1).start()
    put_extra(own_o, packed_own)

    def add(index, step):
        terms, got = backs[index][0], backs[index][2]
        at = both(step)
        terms[at, :] = (terms[at, :].astype(f32) + got[at, :].astype(f32)).astype(bf16)

    def pass_on(index, step):
        if index == 1:
            half_over(step).wait_recv()
        add(index, step)
        for member in range(2):
            back(index, step, member).start()

    def pass_all(index):
        loop(1, couples, lambda step: pass_on(index, step))
        if index == 1:
            half_over(0).wait_recv()
        add(index, 0)
        back(index, 0, 1 - me % 2).start()
        back_here(index).start()

    for part in range(PARTS + 1):
        for side in range(2):
            piece_over(part, side).wait_recv()
    pass_all(0)
    to_terms([d_gate, d_up], [0, 1], tensor, own_i)
    pass_all(1)
    factor(1, 1).wait_recv()
    factor(2, 1).start()

    def returned(index):
        back_here(index).wait()
        back_come(index, 0, 1 - me % 2).wait_recv()

        def come(step):
            for member in range(2):
                back_come(index, step, member).wait_recv()

        loop(1, couples, come)
        to = backs[index][3]
        for part in range(2):
            at = part * block + depth
            rest_of(to[:, at : at + LANES], ret_rest, part)
        return [
            jnp.concatenate(
                [
                    to[:, part * block : part * block + depth],
                    ret_rest[:, part * depth : (part + 1) * depth],
                ],
                axis=0,
            )
            for part in range(2)
        ]

    factor(0, 0).wait_recv()
    factor(2, 0).wait_recv()
    weight_grad(2)
    total = None
    for part, values in enumerate(returned(0)):
        at = slice(part * depth, (part + 1) * depth)
        layer_out[:, at] = dot(weighted[...], values).astype(bf16)
        term = dot(cotangent[:, at], values, INNER)
        total = term if total is None else total + term

    line = lax.broadcasted_iota(jnp.int32, (all_rows, LANES), 0)
    column = lax.broadcasted_iota(jnp.int32, (all_rows, LANES), 1)
    owner = jnp.where(line < count, line // TILE, line - count)
    to_owner = (owner == column).astype(f32).astype(bf16)
    left_over = total * select[...].astype(f32)
    sums = None
    for _ in range(3):
        term = left_over.astype(bf16)
        left_over = left_over - term.astype(f32)
        term = dot(term, to_owner)
        sums = term if sums is None else sums + term
    part_scores[...] = sums
    trade = remote(
        part_scores, other_scores, local_sems.at[7], local_sems.at[8], opposite
    )
    trade.start()

    for part, values in enumerate(returned(1)):
        at = slice(part * depth, (part + 1) * depth)
        input_grad[:, at] = dot(select[...], values).astype(bf16)
    factor(0, 1).wait_recv()
    factor(2, 1).wait_recv()
    for index in range(2):
        weight_grad(index)
    trade.wait()
    owner_scores[...] = part_scores[...] + other_scores[...]

    def spread_gone(matrix, part):
        swap(matrix, part).wait_send()
        for kind in range(3):
            spread(matrix, part, kind).wait_send()

    for matrix in range(3):
        loop(0, PARTS, lambda part, matrix=matrix: spread_gone(matrix, part))
    for kind in range(3):
        for late in range(2):
            factor(kind, late).wait_send()
    for part in range(PARTS + 1):
        for side in range(2):
            piece_over(part, side).wait_send()
    loop(0, couples, lambda step: half_over(step).wait_send())
    for index in range(2):
        loop(1, experts, lambda step, index=index: out_slab(index, step).wait_send())
        back(index, 0, 1 - me % 2).wait_send()

        def gone(step, index=index):
            for member in range(2):
                back(index, step, member).wait_send()

        loop(1, couples, gone)
        row_copy(index).wait_send()
        for part in range(2):
            for copy in slice_copies(index, part, 0):
                copy.wait_send()

            @pl.when(dp != tensor * 2 + part)
            def _(index=index, part=part):
                for copy in slice_copies(index, part, 1):
                    copy.wait_send()


def layer(tokens, cotangent, select, weighted, weights, flag):
    experts, replicas, halves = (lax.axis_size(a) for a in ("expert", "dp", "tensor"))
    depth, units = weights[0].shape
    count, all_rows = experts * TILE, experts * CAP
    block, cells = depth + LANES, depth // LANES
    own_rows, half = tokens.shape

    def like(*shape, dtype=jnp.bfloat16):
        return jax.ShapeDtypeStruct(shape, dtype)

    def keep(*shape, dtype=jnp.bfloat16):
        return pltpu.VMEM(shape, dtype)

    out_shape = (
        like(own_rows, half),
        like(own_rows, half),
        like(own_rows, LANES, dtype=jnp.float32),
    ) + (like(depth, units),) * 3
    dma = pltpu.SemaphoreType.DMA
    return pl.pallas_call(
        functools.partial(layer_kernel, experts, replicas, halves),
        name="layer",
        out_shape=out_shape,
        in_specs=[WHOLE] * 4 + [ANY] * 3 + [WHOLE],
        out_specs=(WHOLE,) * len(out_shape),
        scratch_shapes=[keep(count, 2 * block)] * 2
        + [keep(halves, count, 2 * block)] * 2
        + [keep(experts, halves * half)] * 2
        + [keep(replicas * all_rows, depth)] * 2
        + [keep(replicas * count, LANES)] * 2
        + [keep(3, depth, units)]
        + [keep(replicas * depth, units)] * 3
        + [
            keep(3, all_rows, units, dtype=jnp.float32),
            keep(replicas * all_rows, 3 * units),
        ]
        + [keep(cells * experts, 2 * LANES)] * 3
        + [keep(count, 2 * block)] * 8
        + [keep(experts, half)]
        + [keep(own_rows, LANES, dtype=jnp.float32)] * 2
        + [
            dma((2, 2, experts)),
            dma((2, 2)),
            dma((2, 2, 4, 2)),
            dma((4, 3, PARTS, 2)),
            dma((2, experts // 2)),
            dma((2, 2 * PARTS + 2)),
            dma((2, 2, experts)),
            dma((2, 3, 2)),
            dma((9,)),
        ],
        compiler_params=pltpu.CompilerParams(
            collective_id=0, has_side_effects=True, vmem_limit_bytes=60 << 20
        ),
    )(tokens, cotangent, select, weighted, *weights, flag)


def copy_kernel(number, *refs):
    copies = [
        pltpu.make_async_copy(refs[at], refs[number + at], refs[2 * number].at[at])
        for at in range(number)
    ]
    for copy in copies:
        copy.start()
    for copy in copies:
        copy.wait()


def copied(*arrays):
    number = len(arrays)
    return pl.pallas_call(
        functools.partial(copy_kernel, number),
        name="copy_out",
        out_shape=tuple(jax.ShapeDtypeStruct(a.shape, a.dtype) for a in arrays),
        in_specs=[ANY] * number,
        out_specs=(ANY,) * number,
        scratch_shapes=[pltpu.SemaphoreType.DMA((number,))],
    )(*arrays)


def on_device(tokens, routes, gates, cotangent, placement, swap_flag, w_gate, w_up, w_down):
    experts = lax.axis_size("expert")
    myself = lax.axis_index("expert")
    places = jnp.arange(experts, dtype=jnp.int32)
    partner = (places + experts // 2) % experts
    source = jnp.where(swap_flag == 1, partner, places)
    my_flag = jnp.sum(jnp.where(places == myself, swap_flag, 0)) == 1
    held = jnp.sum(jnp.where(source[:, None] == places[None, :], placement[None, :], 0), axis=1)
    tok_count, top_count = routes.shape
    slots_all = experts * CAP
    pair_owner = routes[:, :, None] == held[None, None, :]
    named = jnp.any(pair_owner, axis=1)
    gate_of = jnp.sum(jnp.where(pair_owner, gates[:, :, None].astype(jnp.float32), 0.0), axis=1)
    before = jnp.arange(tok_count)[:, None] > jnp.arange(tok_count)[None, :]
    earlier = jnp.dot(
        before.astype(jnp.bfloat16), named.astype(jnp.bfloat16), preferred_element_type=jnp.float32
    ).astype(jnp.int32)
    rank = jnp.where(named, earlier, CAP)
    column = jnp.arange(slots_all, dtype=jnp.int32)
    in_main = column < experts * TILE
    column_owner = jnp.where(in_main, column // TILE, column - experts * TILE)
    column_slot = jnp.where(in_main, column % TILE, TILE)
    spread = (places[:, None] == column_owner[None, :]).astype(jnp.bfloat16)
    column_rank = jnp.dot(rank.astype(jnp.bfloat16), spread, preferred_element_type=jnp.float32)
    match = column_rank == column_slot[None, :].astype(jnp.float32)
    select = match.astype(jnp.bfloat16)
    column_gate = jnp.dot(gate_of.astype(jnp.bfloat16), spread, preferred_element_type=jnp.float32)
    weighted = jnp.where(match, column_gate, 0.0).astype(jnp.bfloat16)
    flag = jnp.full((TILE, w_gate.shape[2]), my_flag, jnp.float32)
    layer_out, input_grad, owner_scores, *grads = layer(
        tokens, cotangent, select, weighted, (w_gate[0], w_up[0], w_down[0]), flag
    )
    gate_grad = jnp.sum(
        jnp.where(pair_owner, owner_scores[:, None, :experts], 0.0), axis=2
    )
    layer_out, input_grad, *grads = copied(layer_out, input_grad, *grads)
    return (layer_out, input_grad, gate_grad, *(grad[None] for grad in grads))


def solution(mesh):
    placed = (
        P(("expert", "dp"), "tensor"),
        P(("expert", "dp"), None),
        P(("expert", "dp"), None),
        P(("expert", "dp"), "tensor"),
        P(),
        P(),
        P("expert", "dp", "tensor"),
        P("expert", "dp", "tensor"),
        P("expert", "dp", "tensor"),
    )
    return jax.shard_map(
        on_device,
        mesh=mesh,
        in_specs=placed,
        out_specs=(
            P(("expert", "dp"), "tensor"),
            P(("expert", "dp"), "tensor"),
            P(("expert", "dp"), None),
            P("expert", "dp", "tensor"),
            P("expert", "dp", "tensor"),
            P("expert", "dp", "tensor"),
        ),
        check_vma=False,
    )
```

```python
import functools

import jax
import jax.numpy as jnp
from jax import lax
from jax.experimental import pallas as pl
from jax.experimental.pallas import tpu as pltpu
from jax.sharding import PartitionSpec as P

CAP = 9
TILE = 8
LANES = 128
PARTS = 7
MESH = pl.DeviceIdType.MESH
ANY = pl.BlockSpec(memory_space=pl.ANY)
WHOLE = pl.BlockSpec(memory_space=pltpu.VMEM)
CONTRACT = (((0,), (0,)), ((), ()))
INNER = (((1,), (1,)), ((), ()))
PLAIN = (((1,), (0,)), ((), ()))


def dot(left, right, dims=PLAIN):
    return lax.dot_general(left, right, dims, preferred_element_type=jnp.float32)


def remote(src, dst, sent, got, where):
    return pltpu.make_async_remote_copy(
        src_ref=src,
        dst_ref=dst,
        send_sem=sent,
        recv_sem=got,
        device_id=where,
        device_id_type=MESH,
    )


def loop(start, stop, body):
    def step(index, carry):
        body(index)
        return carry

    lax.fori_loop(start, stop, step, 0)


def layer_kernel(
    experts, replicas, halves,
    tokens, cotangent, select, weighted, wg, wu, wd, flag,
    layer_out, input_grad, owner_scores, grad_g, grad_u, grad_d,
    x_pack, g_pack, xh, gh, x_rest, g_rest, x_slice, g_slice, x_extra, g_extra,
    arriving, wgf, wuf, wdf, pre, facs, packed, packed_far, packed_own, own_o, far_o, got_o, own_i, far_i, got_i,
    ret_o, ret_i, ret_rest, part_scores, other_scores,
    a2a_sems, row_sems, slice_sems, weight_sems, tensor_sems, piece_sems, back_sems, factor_sems, local_sems,
):
    me, dp, tensor = lax.axis_index("expert"), lax.axis_index("dp"), lax.axis_index("tensor")
    depth, units = wg.shape
    count = experts * TILE
    all_rows = experts * CAP
    cells = depth // LANES
    block = depth + LANES
    piece = depth // PARTS
    own, full = (wg, wu, wd), (wgf, wuf, wdf)
    sibling = {"dp": dp + 1 - 2 * (dp % 2)}
    across_dp = (dp + 2) % replicas
    across = {"dp": across_dp}
    far = 1 - tensor
    opposite = {"tensor": far}
    bf16, f32 = jnp.bfloat16, jnp.float32

    barrier = pltpu.get_barrier_semaphore()
    group = replicas * halves

    def along(step):
        pl.semaphore_signal(
            barrier, inc=1, device_id={"expert": (me + step) % experts}, device_id_type=MESH
        )

    def inside(step):
        other = (dp * halves + tensor + step) % group
        pl.semaphore_signal(
            barrier,
            inc=1,
            device_id={"dp": other // halves, "tensor": other % halves},
            device_id_type=MESH,
        )

    loop(1, experts, along)
    loop(1, group, inside)

    wide = cells * experts
    line = lax.broadcasted_iota(jnp.int32, (wide, count), 0)
    place = lax.broadcasted_iota(jnp.int32, (wide, count), 1)
    unpacking = ((line % experts) * TILE + line // experts == place).astype(f32).astype(bf16)
    line = lax.broadcasted_iota(jnp.int32, (count, wide), 1)
    place = lax.broadcasted_iota(jnp.int32, (count, wide), 0)
    packing = ((line % experts) * TILE + line // experts == place).astype(f32).astype(bf16)

    def slab(which):
        return pl.ds(pl.multiple_of(which * TILE, TILE), TILE)

    def put(values, index, target):
        target[:, index * block : index * block + depth] = values[:count]
        for cell in range(cells):
            packed[cell * experts : (cell + 1) * experts, index * LANES : (index + 1) * LANES] = (
                values[count:, cell * LANES : (cell + 1) * LANES]
            )

    def put_extra(target, packed=packed):
        extra = dot(packing, packed[...]).astype(bf16)
        for index in range(2):
            target[:, index * block + depth : (index + 1) * block] = extra[
                :, index * LANES : (index + 1) * LANES
            ]

    def rest_of(extra, target, index, first=0):
        rows = dot(unpacking, extra).astype(bf16)
        for cell in range(cells):
            column = index * depth + cell * LANES
            target[first : first + experts, column : column + LANES] = rows[
                cell * experts : (cell + 1) * experts
            ]

    def rows(part):
        return pl.ds(pl.multiple_of(part * piece, 64), piece)

    def region(which, part):
        return pl.ds(pl.multiple_of(which * depth + part * piece, 64), piece)

    def swap(matrix, part):
        sems = weight_sems.at[0, matrix, part]
        return remote(
            own[matrix].at[rows(part)], arriving.at[matrix, rows(part)],
            sems.at[0], sems.at[1], {"expert": (me + experts // 2) % experts},
        )

    def stay(matrix):
        mine = pl.ds(pl.multiple_of(dp * depth, 64), depth)
        return pltpu.make_async_copy(own[matrix], full[matrix].at[mine], local_sems.at[2 + matrix])

    def spread(matrix, part, kind):
        at = region(across_dp if kind == 2 else dp, part)
        sems = weight_sems.at[1 + kind, matrix, part]
        return remote(
            full[matrix].at[at], full[matrix].at[at], sems.at[0], sems.at[1],
            across if kind == 1 else sibling,
        )

    sides = (
        (tokens, select, x_pack, xh, x_slice, x_extra),
        (cotangent, weighted, g_pack, gh, g_slice, g_extra),
    )

    def out_slab(index, step):
        pack, to = sides[index][2:4]
        peer = (me + step) % experts
        return remote(
            pack.at[slab(peer)], to.at[tensor, slab(me)],
            a2a_sems.at[index, 0, step], a2a_sems.at[index, 1, step], {"expert": peer},
        )

    def own_slab(index):
        pack, to = sides[index][2:4]
        return pltpu.make_async_copy(
            pack.at[slab(me)], to.at[tensor, slab(me)], local_sems.at[index]
        )

    for matrix in range(3):
        stay(matrix).start()
    def fill(index):
        data, picks, pack = sides[index][:3]
        for part in range(2):
            values = dot(picks[...], data[:, part * depth : (part + 1) * depth], CONTRACT)
            put(values.astype(bf16), part, pack)
        put_extra(pack)

    def send_rows(index):
        own_slab(index).start()
        loop(1, experts, lambda step: out_slab(index, step).start())

    def send_weights(matrix):
        loop(0, PARTS, lambda part: swap(matrix, part).start())

    fill(0)
    pl.semaphore_wait(barrier, experts - 1 + group - 1)
    send_rows(0)
    fill(1)
    send_rows(1)

    def row_copy(index):
        to = sides[index][3]
        return remote(
            to.at[tensor], to.at[tensor], row_sems.at[index, 0], row_sems.at[index, 1], opposite
        )

    level = dp // 2

    def slice_copies(index, kind):
        to, main, extra = sides[index][3:]
        target, where = (sibling["dp"] if kind == 2 else dp), sibling
        if kind < 2:
            target = 2 * (1 - level) + kind
            where = {"dp": target, "tensor": far}
        start = pl.multiple_of((target % 2) * block, LANES)
        sources = (
            to.at[target // 2, :, pl.ds(start, depth)],
            to.at[target // 2, :, pl.ds(pl.multiple_of(start + depth, LANES), LANES)],
        )
        places = (
            main.at[pl.ds(pl.multiple_of(dp * all_rows, 32), count)],
            extra.at[pl.ds(pl.multiple_of(dp * count, 32), count)],
        )
        got = slice_sems.at[index, 1, dp]
        if kind == 3:
            return [
                pltpu.make_async_copy(sources[number], places[number], got.at[number])
                for number in range(2)
            ]
        sent = slice_sems.at[index, 0, kind]
        return [
            remote(sources[number], places[number], sent.at[number], got.at[number], where)
            for number in range(2)
        ]

    def send_slices(index):
        row_copy(index).wait_recv()
        for kind in range(4):
            for copy in slice_copies(index, kind):
                copy.start()

    def rows_over(index):
        own_slab(index).wait()
        loop(1, experts, lambda step: out_slab(index, step).wait_recv())
        row_copy(index).start()

    def forward(matrix, part):
        spread(matrix, part, 1).wait_recv()
        spread(matrix, part, 2).start()

    def complete(matrix):
        def here(part):
            spread(matrix, part, 0).wait_recv()
            spread(matrix, part, 2).wait_recv()

        loop(0, PARTS, here)

    def unpack_rows(index):
        to, rest = sides[index][3], (x_rest, g_rest)[index]
        for number in range(2 * halves):
            at = (number % 2) * block + depth
            rest_of(to[number // 2, :, at : at + LANES], rest, number)

    def project(index, matrix):
        to, rest = sides[index][3], (x_rest, g_rest)[index]
        for number in range(2 * halves):
            at = (number % 2) * block
            left = jnp.concatenate(
                [
                    to[number // 2, :, at : at + depth],
                    rest[:, number * depth : (number + 1) * depth],
                ],
                axis=0,
            )
            term = dot(left, full[matrix][number * depth : (number + 1) * depth, :])
            pre[matrix] = term if number == 0 else pre[matrix] + term

    strip = 32

    def factor_rows(step):
        return pl.ds(pl.multiple_of(dp * all_rows + step * strip, 32), strip)

    def hide(step):
        lines = pl.ds(pl.multiple_of(step * strip, strip), strip)
        gate, up = pre[0, lines, :], pre[1, lines, :]
        facs[factor_rows(step), 2 * units :] = (gate * jax.nn.sigmoid(gate) * up).astype(bf16)

    def to_terms(lefts, matrices, which, target):
        for part in range(2):
            at = pl.ds(pl.multiple_of((which * 2 + part) * depth, 64), depth)
            terms = None
            for left, matrix in zip(lefts, matrices):
                term = dot(left, full[matrix][at, :], INNER)
                terms = term if terms is None else terms + term
            put(terms.astype(bf16), part, target)
        put_extra(target)

    backs = ((own_o, far_o, got_o, ret_o), (own_i, far_i, got_i, ret_i))

    couples = experts // 2

    def couple(step):
        return (me // 2 + step) % couples

    def both(step):
        return pl.ds(pl.multiple_of(couple(step) * 2 * TILE, 2 * TILE), 2 * TILE)

    def half_over(step):
        return remote(
            far_i.at[both(step)], got_i.at[both(step)],
            tensor_sems.at[0, step], tensor_sems.at[1, step], opposite,
        )

    def back(index, step, member):
        terms, to = backs[index][0], backs[index][3]
        peer = couple(step) * 2 + member
        return remote(
            terms.at[slab(peer)], to.at[slab(me)],
            back_sems.at[index, 0, 2 * step + member], back_sems.at[index, 1, 2 * step + me % 2],
            {"expert": peer},
        )

    def back_come(index, step, member):
        terms, to = backs[index][0], backs[index][3]
        peer = couple(step) * 2 + member
        return remote(
            terms.at[slab(peer)], to.at[slab(me)],
            back_sems.at[index, 0, 2 * step + member], back_sems.at[index, 1, 2 * step + member],
            {"expert": peer},
        )

    def back_here(index):
        terms, to = backs[index][0], backs[index][3]
        return pltpu.make_async_copy(terms.at[slab(me)], to.at[slab(me)], local_sems.at[5 + index])

    def factor(kind, late):
        which = across_dp if kind == 2 else dp
        at = pl.ds(pl.multiple_of(which * all_rows, 32), all_rows)
        cut = slice(0, 2 * units) if late else slice(2 * units, 3 * units)
        sems = factor_sems.at[late, kind]
        return remote(
            facs.at[at, cut], facs.at[at, cut], sems.at[0], sems.at[1],
            across if kind == 1 else sibling,
        )

    def slices_landed(index):
        to, main, extra = sides[index][3:]

        def landed(source):
            got = slice_sems.at[index, 1, source]
            at = pl.ds(pl.multiple_of(source * all_rows, 32), count)
            pltpu.make_async_copy(main.at[at], main.at[at], got.at[0]).wait()
            at = pl.ds(pl.multiple_of(source * count, 32), count)
            pltpu.make_async_copy(extra.at[at], extra.at[at], got.at[1]).wait()

        loop(0, replicas, landed)
        for source in range(replicas):
            rest_of(
                extra[source * count : (source + 1) * count, :],
                main,
                0,
                source * all_rows + count,
            )

    def weight_grad(index):
        left, grad = ((x_slice, grad_g), (x_slice, grad_u), (g_slice, grad_d))[index]
        right = facs[:, index * units : (index + 1) * units]
        cuts = (0, 512, depth) if depth > 512 else (0, depth)
        for low, high in zip(cuts, cuts[1:]):
            grad[low:high, :] = dot(left[:, low:high], right, CONTRACT).astype(bf16)

    mine = pl.ds(pl.multiple_of(dp * all_rows, 32), all_rows)
    taken = flag[0:1, :]

    def take(matrix, part):
        swap(matrix, part).wait_recv()
        for step in range(piece // 64):
            lines = pl.ds(pl.multiple_of(part * piece + step * 64, 64), 64)
            at = pl.ds(pl.multiple_of(dp * depth + part * piece + step * 64, 64), 64)
            fresh = arriving[matrix, lines, :].astype(f32)
            former = full[matrix][at, :].astype(f32)
            full[matrix][at, :] = (fresh * taken + former * (1.0 - taken)).astype(bf16)
        spread(matrix, part, 1).start()
        spread(matrix, part, 0).start()

    def take_and_forward(matrix, part):
        take(matrix, part)
        forward(matrix, part - 1)

    def piece_over(part, side):
        at = side * block + part * piece
        number = 2 * part + side
        return remote(
            far_o.at[:, at : at + piece], got_o.at[:, at : at + piece],
            piece_sems.at[0, number], piece_sems.at[1, number], opposite,
        )

    def use_down(part):
        spread(2, part, 0).wait_recv()
        spread(2, part, 2).wait_recv()
        hidden = facs[mine, 2 * units :]
        low = part * piece
        for which, target, wide_form in ((far, far_o, packed_far), (tensor, own_o, packed_own)):
            for side in range(2):
                at = pl.ds(pl.multiple_of((which * 2 + side) * depth + low, 64), piece)
                values = dot(hidden, full[2][at, :], INNER).astype(bf16)
                target[:, side * block + low : side * block + low + piece] = values[:count]
                for cell in range(piece // LANES):
                    line = (low // LANES + cell) * experts
                    wide_form[line : line + experts, side * LANES : (side + 1) * LANES] = values[
                        count:, cell * LANES : (cell + 1) * LANES
                    ]
            if target is far_o:
                for side in range(2):
                    piece_over(part, side).start()
        total = None
        for number in range(2 * halves):
            at = (number % 2) * block + low
            left = jnp.concatenate(
                [
                    gh[number // 2, :, at : at + piece],
                    g_rest[:, number * depth + low : number * depth + low + piece],
                ],
                axis=0,
            )
            at = number * depth + low
            term = dot(left, full[2][at : at + piece, :])
            total = term if total is None else total + term
        pre[2] = total if part == 0 else pre[2] + total

    for matrix in range(3):
        send_weights(matrix)
    rows_over(0)
    rows_over(1)
    stay(0).wait()
    take(0, 0)
    loop(1, PARTS // 2, lambda part: take_and_forward(0, part))
    send_slices(0)
    loop(PARTS // 2, PARTS, lambda part: take_and_forward(0, part))
    stay(1).wait()
    take(1, 0)
    forward(0, PARTS - 1)
    send_slices(1)
    loop(1, PARTS, lambda part: take_and_forward(1, part))
    stay(2).wait()
    for part in range(PARTS):
        take(2, part)
        forward(*((1, PARTS - 1) if part == 0 else (2, part - 1)))
        if part == 0:
            unpack_rows(0)
            complete(0)
            project(0, 0)
        if part == 1:
            unpack_rows(1)
        if part == 2:
            complete(1)
            project(0, 1)
            loop(0, all_rows // strip, hide)
            factor(1, 0).start()
            factor(0, 0).start()
        if part == 3:
            slices_landed(0)
        if part == 5:
            factor(1, 0).wait_recv()
            factor(2, 0).start()
        if part >= 2:
            use_down(part - 2)
    forward(2, PARTS - 1)
    use_down(PARTS - 2)
    use_down(PARTS - 1)
    put_extra(far_o, packed_far)
    for side in range(2):
        piece_over(PARTS, side).start()

    def differentiate(step):
        lines = pl.ds(pl.multiple_of(step * strip, strip), strip)
        gate, up, d_hidden = pre[0, lines, :], pre[1, lines, :], pre[2, lines, :]
        sig = jax.nn.sigmoid(gate)
        at = factor_rows(step)
        facs[at, :units] = (d_hidden * up * sig * (1.0 + gate * (1.0 - sig))).astype(bf16)
        facs[at, units : 2 * units] = (d_hidden * gate * sig).astype(bf16)

    loop(0, all_rows // strip, differentiate)
    d_gate, d_up = facs[mine, :units], facs[mine, units : 2 * units]
    to_terms([d_gate, d_up], [0, 1], far, far_i)
    loop(0, couples, lambda step: half_over(step).start())
    factor(1, 1).start()
    factor(0, 1).start()
    put_extra(own_o, packed_own)

    def add(index, step):
        terms, got = backs[index][0], backs[index][2]
        at = both(step)
        terms[at, :] = (terms[at, :].astype(f32) + got[at, :].astype(f32)).astype(bf16)

    def pass_on(index, step):
        if index == 1:
            half_over(step).wait_recv()
        add(index, step)
        for member in range(2):
            back(index, step, member).start()

    def pass_all(index):
        loop(1, couples, lambda step: pass_on(index, step))
        if index == 1:
            half_over(0).wait_recv()
        add(index, 0)
        back(index, 0, 1 - me % 2).start()
        back_here(index).start()

    for part in range(PARTS + 1):
        for side in range(2):
            piece_over(part, side).wait_recv()
    pass_all(0)
    to_terms([d_gate, d_up], [0, 1], tensor, own_i)
    pass_all(1)
    factor(1, 1).wait_recv()
    factor(2, 1).start()

    def returned(index):
        back_here(index).wait()
        back_come(index, 0, 1 - me % 2).wait_recv()

        def come(step):
            for member in range(2):
                back_come(index, step, member).wait_recv()

        loop(1, couples, come)
        to = backs[index][3]
        for part in range(2):
            at = part * block + depth
            rest_of(to[:, at : at + LANES], ret_rest, part)
        return [
            jnp.concatenate(
                [
                    to[:, part * block : part * block + depth],
                    ret_rest[:, part * depth : (part + 1) * depth],
                ],
                axis=0,
            )
            for part in range(2)
        ]

    slices_landed(1)
    factor(0, 0).wait_recv()
    factor(2, 0).wait_recv()
    weight_grad(2)
    total = None
    for part, values in enumerate(returned(0)):
        at = slice(part * depth, (part + 1) * depth)
        layer_out[:, at] = dot(weighted[...], values).astype(bf16)
        term = dot(cotangent[:, at], values, INNER)
        total = term if total is None else total + term

    line = lax.broadcasted_iota(jnp.int32, (all_rows, LANES), 0)
    column = lax.broadcasted_iota(jnp.int32, (all_rows, LANES), 1)
    owner = jnp.where(line < count, line // TILE, line - count)
    to_owner = (owner == column).astype(f32).astype(bf16)
    left_over = total * select[...].astype(f32)
    sums = None
    for _ in range(3):
        term = left_over.astype(bf16)
        left_over = left_over - term.astype(f32)
        term = dot(term, to_owner)
        sums = term if sums is None else sums + term
    part_scores[...] = sums
    trade = remote(
        part_scores, other_scores, local_sems.at[7], local_sems.at[8], opposite
    )
    trade.start()

    for part, values in enumerate(returned(1)):
        at = slice(part * depth, (part + 1) * depth)
        input_grad[:, at] = dot(select[...], values).astype(bf16)
    factor(0, 1).wait_recv()
    factor(2, 1).wait_recv()
    for index in range(2):
        weight_grad(index)
    trade.wait()
    owner_scores[...] = part_scores[...] + other_scores[...]

    def spread_gone(matrix, part):
        swap(matrix, part).wait_send()
        for kind in range(3):
            spread(matrix, part, kind).wait_send()

    for matrix in range(3):
        loop(0, PARTS, lambda part, matrix=matrix: spread_gone(matrix, part))
    for kind in range(3):
        for late in range(2):
            factor(kind, late).wait_send()
    for part in range(PARTS + 1):
        for side in range(2):
            piece_over(part, side).wait_send()
    loop(0, couples, lambda step: half_over(step).wait_send())
    for index in range(2):
        loop(1, experts, lambda step, index=index: out_slab(index, step).wait_send())
        back(index, 0, 1 - me % 2).wait_send()

        def gone(step, index=index):
            for member in range(2):
                back(index, step, member).wait_send()

        loop(1, couples, gone)
        row_copy(index).wait_send()
        for kind in range(3):
            for copy in slice_copies(index, kind):
                copy.wait_send()


def layer(tokens, cotangent, select, weighted, weights, flag):
    experts, replicas, halves = (lax.axis_size(a) for a in ("expert", "dp", "tensor"))
    depth, units = weights[0].shape
    count, all_rows = experts * TILE, experts * CAP
    block, cells = depth + LANES, depth // LANES
    own_rows, half = tokens.shape

    def like(*shape, dtype=jnp.bfloat16):
        return jax.ShapeDtypeStruct(shape, dtype)

    def keep(*shape, dtype=jnp.bfloat16):
        return pltpu.VMEM(shape, dtype)

    out_shape = (
        like(own_rows, half),
        like(own_rows, half),
        like(own_rows, LANES, dtype=jnp.float32),
    ) + (like(depth, units),) * 3
    dma = pltpu.SemaphoreType.DMA
    return pl.pallas_call(
        functools.partial(layer_kernel, experts, replicas, halves),
        name="layer",
        out_shape=out_shape,
        in_specs=[WHOLE] * 4 + [ANY] * 3 + [WHOLE],
        out_specs=(WHOLE,) * len(out_shape),
        scratch_shapes=[keep(count, 2 * block)] * 2
        + [keep(halves, count, 2 * block)] * 2
        + [keep(experts, halves * half)] * 2
        + [keep(replicas * all_rows, depth)] * 2
        + [keep(replicas * count, LANES)] * 2
        + [keep(3, depth, units)]
        + [keep(replicas * depth, units)] * 3
        + [
            keep(3, all_rows, units, dtype=jnp.float32),
            keep(replicas * all_rows, 3 * units),
        ]
        + [keep(cells * experts, 2 * LANES)] * 3
        + [keep(count, 2 * block)] * 8
        + [keep(experts, half)]
        + [keep(own_rows, LANES, dtype=jnp.float32)] * 2
        + [
            dma((2, 2, experts)),
            dma((2, 2)),
            dma((2, 2, 4, 2)),
            dma((4, 3, PARTS, 2)),
            dma((2, experts // 2)),
            dma((2, 2 * PARTS + 2)),
            dma((2, 2, experts)),
            dma((2, 3, 2)),
            dma((9,)),
        ],
        compiler_params=pltpu.CompilerParams(
            collective_id=0, has_side_effects=True, vmem_limit_bytes=60 << 20
        ),
    )(tokens, cotangent, select, weighted, *weights, flag)


def copy_kernel(number, *refs):
    ins, outs, keeps, sems = (refs[:number], refs[number : 2 * number], refs[2 * number : -1], refs[-1])
    arrive = [
        pltpu.make_async_copy(ins[at], keeps[at], sems.at[0, at]) for at in range(number)
    ]
    leave = [
        pltpu.make_async_copy(keeps[at], outs[at], sems.at[1, at]) for at in range(number)
    ]
    for copy in arrive:
        copy.start()
    for first, second in zip(arrive, leave):
        first.wait()
        second.start()
    for copy in leave:
        copy.wait()


def copied(*arrays):
    number = len(arrays)
    return pl.pallas_call(
        functools.partial(copy_kernel, number),
        name="copy_out",
        out_shape=tuple(jax.ShapeDtypeStruct(a.shape, a.dtype) for a in arrays),
        in_specs=[ANY] * number,
        out_specs=(ANY,) * number,
        scratch_shapes=[pltpu.VMEM(a.shape, a.dtype) for a in arrays]
        + [pltpu.SemaphoreType.DMA((2, number))],
        compiler_params=pltpu.CompilerParams(vmem_limit_bytes=60 << 20),
    )(*arrays)


def on_device(tokens, routes, gates, cotangent, placement, swap_flag, w_gate, w_up, w_down):
    experts = lax.axis_size("expert")
    myself = lax.axis_index("expert")
    places = jnp.arange(experts, dtype=jnp.int32)
    partner = (places + experts // 2) % experts
    source = jnp.where(swap_flag == 1, partner, places)
    my_flag = jnp.sum(jnp.where(places == myself, swap_flag, 0)) == 1
    held = jnp.sum(jnp.where(source[:, None] == places[None, :], placement[None, :], 0), axis=1)
    tok_count, top_count = routes.shape
    slots_all = experts * CAP
    pair_owner = routes[:, :, None] == held[None, None, :]
    named = jnp.any(pair_owner, axis=1)
    gate_of = jnp.sum(jnp.where(pair_owner, gates[:, :, None].astype(jnp.float32), 0.0), axis=1)
    before = jnp.arange(tok_count)[:, None] > jnp.arange(tok_count)[None, :]
    earlier = jnp.dot(
        before.astype(jnp.bfloat16), named.astype(jnp.bfloat16), preferred_element_type=jnp.float32
    ).astype(jnp.int32)
    rank = jnp.where(named, earlier, CAP)
    column = jnp.arange(slots_all, dtype=jnp.int32)
    in_main = column < experts * TILE
    column_owner = jnp.where(in_main, column // TILE, column - experts * TILE)
    column_slot = jnp.where(in_main, column % TILE, TILE)
    spread = (places[:, None] == column_owner[None, :]).astype(jnp.bfloat16)
    column_rank = jnp.dot(rank.astype(jnp.bfloat16), spread, preferred_element_type=jnp.float32)
    match = column_rank == column_slot[None, :].astype(jnp.float32)
    select = match.astype(jnp.bfloat16)
    column_gate = jnp.dot(gate_of.astype(jnp.bfloat16), spread, preferred_element_type=jnp.float32)
    weighted = jnp.where(match, column_gate, 0.0).astype(jnp.bfloat16)
    flag = jnp.full((TILE, w_gate.shape[2]), my_flag, jnp.float32)
    layer_out, input_grad, owner_scores, *grads = layer(
        tokens, cotangent, select, weighted, (w_gate[0], w_up[0], w_down[0]), flag
    )
    gate_grad = jnp.sum(
        jnp.where(pair_owner, owner_scores[:, None, :experts], 0.0), axis=2
    )
    layer_out, input_grad, *grads = copied(layer_out, input_grad, *grads)
    return (layer_out, input_grad, gate_grad, *(grad[None] for grad in grads))


def solution(mesh):
    placed = (
        P(("expert", "dp"), "tensor"),
        P(("expert", "dp"), None),
        P(("expert", "dp"), None),
        P(("expert", "dp"), "tensor"),
        P(),
        P(),
        P("expert", "dp", "tensor"),
        P("expert", "dp", "tensor"),
        P("expert", "dp", "tensor"),
    )
    return jax.shard_map(
        on_device,
        mesh=mesh,
        in_specs=placed,
        out_specs=(
            P(("expert", "dp"), "tensor"),
            P(("expert", "dp"), "tensor"),
            P(("expert", "dp"), None),
            P("expert", "dp", "tensor"),
            P("expert", "dp", "tensor"),
            P("expert", "dp", "tensor"),
        ),
        check_vma=False,
    )
```

```python
import functools

import jax
import jax.numpy as jnp
from jax import lax
from jax.experimental import pallas as pl
from jax.experimental.pallas import tpu as pltpu
from jax.sharding import PartitionSpec as P

CAP = 9
TILE = 8
LANES = 128
PARTS = 7
MESH = pl.DeviceIdType.MESH
ANY = pl.BlockSpec(memory_space=pl.ANY)
WHOLE = pl.BlockSpec(memory_space=pltpu.VMEM)
CONTRACT = (((0,), (0,)), ((), ()))
INNER = (((1,), (1,)), ((), ()))
PLAIN = (((1,), (0,)), ((), ()))


def dot(left, right, dims=PLAIN):
    return lax.dot_general(left, right, dims, preferred_element_type=jnp.float32)


def remote(src, dst, sent, got, where):
    return pltpu.make_async_remote_copy(
        src_ref=src,
        dst_ref=dst,
        send_sem=sent,
        recv_sem=got,
        device_id=where,
        device_id_type=MESH,
    )


def loop(start, stop, body):
    def step(index, carry):
        body(index)
        return carry

    lax.fori_loop(start, stop, step, 0)


def layer_kernel(
    experts, replicas, halves,
    tokens, cotangent, select, weighted, wg, wu, wd, flag,
    layer_out, input_grad, owner_scores, grad_g, grad_u, grad_d,
    x_pack, g_pack, xh, gh, x_rest, g_rest, x_slice, g_slice, x_extra, g_extra,
    arriving, wgf, wuf, wdf, pre, facs, packed, packed_far, packed_own, own_o, far_o, got_o, own_i, far_i, got_i,
    ret_o, ret_i, ret_rest, part_scores, other_scores,
    a2a_sems, row_sems, slice_sems, weight_sems, tensor_sems, piece_sems, back_sems, factor_sems, local_sems,
):
    me, dp, tensor = lax.axis_index("expert"), lax.axis_index("dp"), lax.axis_index("tensor")
    depth, units = wg.shape
    count = experts * TILE
    all_rows = experts * CAP
    cells = depth // LANES
    block = depth + LANES
    piece = depth // PARTS
    own, full = (wg, wu, wd), (wgf, wuf, wdf)
    sibling = {"dp": dp + 1 - 2 * (dp % 2)}
    across_dp = (dp + 2) % replicas
    across = {"dp": across_dp}
    far = 1 - tensor
    opposite = {"tensor": far}
    bf16, f32 = jnp.bfloat16, jnp.float32

    barrier = pltpu.get_barrier_semaphore()
    group = replicas * halves

    def along(step):
        pl.semaphore_signal(
            barrier, inc=1, device_id={"expert": (me + step) % experts}, device_id_type=MESH
        )

    def inside(step):
        other = (dp * halves + tensor + step) % group
        pl.semaphore_signal(
            barrier,
            inc=1,
            device_id={"dp": other // halves, "tensor": other % halves},
            device_id_type=MESH,
        )

    loop(1, experts, along)
    loop(1, group, inside)

    wide = cells * experts
    line = lax.broadcasted_iota(jnp.int32, (wide, count), 0)
    place = lax.broadcasted_iota(jnp.int32, (wide, count), 1)
    unpacking = ((line % experts) * TILE + line // experts == place).astype(f32).astype(bf16)
    line = lax.broadcasted_iota(jnp.int32, (count, wide), 1)
    place = lax.broadcasted_iota(jnp.int32, (count, wide), 0)
    packing = ((line % experts) * TILE + line // experts == place).astype(f32).astype(bf16)

    def slab(which):
        return pl.ds(pl.multiple_of(which * TILE, TILE), TILE)

    def put(values, index, target):
        target[:, index * block : index * block + depth] = values[:count]
        for cell in range(cells):
            packed[cell * experts : (cell + 1) * experts, index * LANES : (index + 1) * LANES] = (
                values[count:, cell * LANES : (cell + 1) * LANES]
            )

    def put_extra(target, packed=packed):
        extra = dot(packing, packed[...]).astype(bf16)
        for index in range(2):
            target[:, index * block + depth : (index + 1) * block] = extra[
                :, index * LANES : (index + 1) * LANES
            ]

    def rest_of(extra, target, index, first=0):
        rows = dot(unpacking, extra).astype(bf16)
        for cell in range(cells):
            column = index * depth + cell * LANES
            target[first : first + experts, column : column + LANES] = rows[
                cell * experts : (cell + 1) * experts
            ]

    def rows(part):
        return pl.ds(pl.multiple_of(part * piece, 64), piece)

    def region(which, part):
        return pl.ds(pl.multiple_of(which * depth + part * piece, 64), piece)

    def swap(matrix, part):
        sems = weight_sems.at[0, matrix, part]
        return remote(
            own[matrix].at[rows(part)], arriving.at[matrix, rows(part)],
            sems.at[0], sems.at[1], {"expert": (me + experts // 2) % experts},
        )

    def stay(matrix):
        mine = pl.ds(pl.multiple_of(dp * depth, 64), depth)
        return pltpu.make_async_copy(own[matrix], full[matrix].at[mine], local_sems.at[2 + matrix])

    def spread(matrix, part, kind):
        at = region(across_dp if kind == 2 else dp, part)
        sems = weight_sems.at[1 + kind, matrix, part]
        return remote(
            full[matrix].at[at], full[matrix].at[at], sems.at[0], sems.at[1],
            across if kind == 1 else sibling,
        )

    sides = (
        (tokens, select, x_pack, xh, x_slice, x_extra),
        (cotangent, weighted, g_pack, gh, g_slice, g_extra),
    )

    def out_slab(index, step):
        pack, to = sides[index][2:4]
        peer = (me + step) % experts
        return remote(
            pack.at[slab(peer)], to.at[tensor, slab(me)],
            a2a_sems.at[index, 0, step], a2a_sems.at[index, 1, step], {"expert": peer},
        )

    def own_slab(index):
        pack, to = sides[index][2:4]
        return pltpu.make_async_copy(
            pack.at[slab(me)], to.at[tensor, slab(me)], local_sems.at[index]
        )

    for matrix in range(3):
        stay(matrix).start()
    def fill(index):
        data, picks, pack = sides[index][:3]
        for part in range(2):
            values = dot(picks[...], data[:, part * depth : (part + 1) * depth], CONTRACT)
            put(values.astype(bf16), part, pack)
        put_extra(pack)

    def send_rows(index):
        own_slab(index).start()
        loop(1, experts, lambda step: out_slab(index, step).start())

    def send_weights(matrix):
        loop(0, PARTS, lambda part: swap(matrix, part).start())

    fill(0)
    pl.semaphore_wait(barrier, experts - 1 + group - 1)
    send_rows(0)
    fill(1)
    send_rows(1)

    def row_copy(index):
        to = sides[index][3]
        return remote(
            to.at[tensor], to.at[tensor], row_sems.at[index, 0], row_sems.at[index, 1], opposite
        )

    level = dp // 2

    def slice_copies(index, kind):
        to, main, extra = sides[index][3:]
        target, where = (sibling["dp"] if kind == 2 else dp), sibling
        if kind < 2:
            target = 2 * (1 - level) + kind
            where = {"dp": target, "tensor": far}
        start = pl.multiple_of((target % 2) * block, LANES)
        sources = (
            to.at[target // 2, :, pl.ds(start, depth)],
            to.at[target // 2, :, pl.ds(pl.multiple_of(start + depth, LANES), LANES)],
        )
        places = (
            main.at[pl.ds(pl.multiple_of(dp * all_rows, 32), count)],
            extra.at[pl.ds(pl.multiple_of(dp * count, 32), count)],
        )
        got = slice_sems.at[index, 1, dp]
        if kind == 3:
            return [
                pltpu.make_async_copy(sources[number], places[number], got.at[number])
                for number in range(2)
            ]
        sent = slice_sems.at[index, 0, kind]
        return [
            remote(sources[number], places[number], sent.at[number], got.at[number], where)
            for number in range(2)
        ]

    def send_slices(index):
        row_copy(index).wait_recv()
        for kind in range(4):
            for copy in slice_copies(index, kind):
                copy.start()

    def rows_over(index):
        own_slab(index).wait()
        loop(1, experts, lambda step: out_slab(index, step).wait_recv())
        row_copy(index).start()

    def forward(matrix, part):
        spread(matrix, part, 1).wait_recv()
        spread(matrix, part, 2).start()

    def complete(matrix):
        def here(part):
            spread(matrix, part, 0).wait_recv()
            spread(matrix, part, 2).wait_recv()

        loop(0, PARTS, here)

    def unpack_rows(index):
        to, rest = sides[index][3], (x_rest, g_rest)[index]
        for number in range(2 * halves):
            at = (number % 2) * block + depth
            rest_of(to[number // 2, :, at : at + LANES], rest, number)

    def project(index, matrix):
        to, rest = sides[index][3], (x_rest, g_rest)[index]
        for number in range(2 * halves):
            at = (number % 2) * block
            left = jnp.concatenate(
                [
                    to[number // 2, :, at : at + depth],
                    rest[:, number * depth : (number + 1) * depth],
                ],
                axis=0,
            )
            term = dot(left, full[matrix][number * depth : (number + 1) * depth, :])
            pre[matrix] = term if number == 0 else pre[matrix] + term

    strip = 32

    def factor_rows(step):
        return pl.ds(pl.multiple_of(dp * all_rows + step * strip, 32), strip)

    def hide(step):
        lines = pl.ds(pl.multiple_of(step * strip, strip), strip)
        gate, up = pre[0, lines, :], pre[1, lines, :]
        facs[factor_rows(step), 2 * units :] = (gate * jax.nn.sigmoid(gate) * up).astype(bf16)

    def to_terms(lefts, matrices, which, target):
        for part in range(2):
            at = pl.ds(pl.multiple_of((which * 2 + part) * depth, 64), depth)
            terms = None
            for left, matrix in zip(lefts, matrices):
                term = dot(left, full[matrix][at, :], INNER)
                terms = term if terms is None else terms + term
            put(terms.astype(bf16), part, target)
        put_extra(target)

    backs = ((own_o, far_o, got_o, ret_o), (own_i, far_i, got_i, ret_i))

    couples = experts // 2

    def couple(step):
        return (me // 2 + step) % couples

    def both(step):
        return pl.ds(pl.multiple_of(couple(step) * 2 * TILE, 2 * TILE), 2 * TILE)

    def half_over(step):
        return remote(
            far_i.at[both(step)], got_i.at[both(step)],
            tensor_sems.at[0, step], tensor_sems.at[1, step], opposite,
        )

    def back(index, step, member):
        terms, to = backs[index][0], backs[index][3]
        peer = couple(step) * 2 + member
        return remote(
            terms.at[slab(peer)], to.at[slab(me)],
            back_sems.at[index, 0, 2 * step + member], back_sems.at[index, 1, 2 * step + me % 2],
            {"expert": peer},
        )

    def back_come(index, step, member):
        terms, to = backs[index][0], backs[index][3]
        peer = couple(step) * 2 + member
        return remote(
            terms.at[slab(peer)], to.at[slab(me)],
            back_sems.at[index, 0, 2 * step + member], back_sems.at[index, 1, 2 * step + member],
            {"expert": peer},
        )

    def back_here(index):
        terms, to = backs[index][0], backs[index][3]
        return pltpu.make_async_copy(terms.at[slab(me)], to.at[slab(me)], local_sems.at[5 + index])

    def factor(kind, late):
        which = across_dp if kind == 2 else dp
        at = pl.ds(pl.multiple_of(which * all_rows, 32), all_rows)
        cut = slice(0, 2 * units) if late else slice(2 * units, 3 * units)
        sems = factor_sems.at[late, kind]
        return remote(
            facs.at[at, cut], facs.at[at, cut], sems.at[0], sems.at[1],
            across if kind == 1 else sibling,
        )

    def slices_landed(index):
        to, main, extra = sides[index][3:]

        def landed(source):
            got = slice_sems.at[index, 1, source]
            at = pl.ds(pl.multiple_of(source * all_rows, 32), count)
            pltpu.make_async_copy(main.at[at], main.at[at], got.at[0]).wait()
            at = pl.ds(pl.multiple_of(source * count, 32), count)
            pltpu.make_async_copy(extra.at[at], extra.at[at], got.at[1]).wait()

        loop(0, replicas, landed)
        for source in range(replicas):
            rest_of(
                extra[source * count : (source + 1) * count, :],
                main,
                0,
                source * all_rows + count,
            )

    def weight_grad(index):
        left, grad = ((x_slice, grad_g), (x_slice, grad_u), (g_slice, grad_d))[index]
        right = facs[:, index * units : (index + 1) * units]
        cuts = (0, 512, depth) if depth > 512 else (0, depth)
        for low, high in zip(cuts, cuts[1:]):
            grad[low:high, :] = dot(left[:, low:high], right, CONTRACT).astype(bf16)

    mine = pl.ds(pl.multiple_of(dp * all_rows, 32), all_rows)
    taken = flag[0:1, :]

    def take(matrix, part):
        swap(matrix, part).wait_recv()
        for step in range(piece // 64):
            lines = pl.ds(pl.multiple_of(part * piece + step * 64, 64), 64)
            at = pl.ds(pl.multiple_of(dp * depth + part * piece + step * 64, 64), 64)
            fresh = arriving[matrix, lines, :].astype(f32)
            former = full[matrix][at, :].astype(f32)
            full[matrix][at, :] = (fresh * taken + former * (1.0 - taken)).astype(bf16)
        spread(matrix, part, 1).start()
        spread(matrix, part, 0).start()

    def take_and_forward(matrix, part):
        take(matrix, part)
        forward(matrix, part - 1)

    def piece_over(part, side):
        at = side * block + part * piece
        number = 2 * part + side
        return remote(
            far_o.at[:, at : at + piece], got_o.at[:, at : at + piece],
            piece_sems.at[0, number], piece_sems.at[1, number], opposite,
        )

    def use_down(part):
        spread(2, part, 0).wait_recv()
        spread(2, part, 2).wait_recv()
        hidden = facs[mine, 2 * units :]
        low = part * piece
        for which, target, wide_form in ((far, far_o, packed_far), (tensor, own_o, packed_own)):
            for side in range(2):
                at = pl.ds(pl.multiple_of((which * 2 + side) * depth + low, 64), piece)
                values = dot(hidden, full[2][at, :], INNER).astype(bf16)
                target[:, side * block + low : side * block + low + piece] = values[:count]
                for cell in range(piece // LANES):
                    line = (low // LANES + cell) * experts
                    wide_form[line : line + experts, side * LANES : (side + 1) * LANES] = values[
                        count:, cell * LANES : (cell + 1) * LANES
                    ]
            if target is far_o:
                for side in range(2):
                    piece_over(part, side).start()
        total = None
        for number in range(2 * halves):
            at = (number % 2) * block + low
            left = jnp.concatenate(
                [
                    gh[number // 2, :, at : at + piece],
                    g_rest[:, number * depth + low : number * depth + low + piece],
                ],
                axis=0,
            )
            at = number * depth + low
            term = dot(left, full[2][at : at + piece, :])
            total = term if total is None else total + term
        pre[2] = total if part == 0 else pre[2] + total

    for matrix in range(3):
        send_weights(matrix)
    rows_over(0)
    rows_over(1)
    stay(0).wait()
    take(0, 0)
    loop(1, PARTS // 2, lambda part: take_and_forward(0, part))
    send_slices(0)
    loop(PARTS // 2, PARTS, lambda part: take_and_forward(0, part))
    stay(1).wait()
    take(1, 0)
    forward(0, PARTS - 1)
    send_slices(1)
    loop(1, PARTS, lambda part: take_and_forward(1, part))
    stay(2).wait()
    for part in range(PARTS):
        take(2, part)
        forward(*((1, PARTS - 1) if part == 0 else (2, part - 1)))
        if part == 0:
            unpack_rows(0)
            complete(0)
            project(0, 0)
        if part == 1:
            unpack_rows(1)
        if part == 2:
            complete(1)
            project(0, 1)
            loop(0, all_rows // strip, hide)
            factor(1, 0).start()
            factor(0, 0).start()
        if part == 3:
            slices_landed(0)
        if part == 5:
            factor(1, 0).wait_recv()
            factor(2, 0).start()
        if part >= 2:
            use_down(part - 2)
    forward(2, PARTS - 1)
    use_down(PARTS - 2)
    use_down(PARTS - 1)
    put_extra(far_o, packed_far)
    for side in range(2):
        piece_over(PARTS, side).start()

    def differentiate(step):
        lines = pl.ds(pl.multiple_of(step * strip, strip), strip)
        gate, up, d_hidden = pre[0, lines, :], pre[1, lines, :], pre[2, lines, :]
        sig = jax.nn.sigmoid(gate)
        at = factor_rows(step)
        facs[at, :units] = (d_hidden * up * sig * (1.0 + gate * (1.0 - sig))).astype(bf16)
        facs[at, units : 2 * units] = (d_hidden * gate * sig).astype(bf16)

    loop(0, all_rows // strip, differentiate)
    d_gate, d_up = facs[mine, :units], facs[mine, units : 2 * units]
    to_terms([d_gate, d_up], [0, 1], far, far_i)
    loop(0, couples, lambda step: half_over(step).start())
    factor(1, 1).start()
    factor(0, 1).start()
    put_extra(own_o, packed_own)

    def add(index, step):
        terms, got = backs[index][0], backs[index][2]
        at = both(step)
        terms[at, :] = (terms[at, :].astype(f32) + got[at, :].astype(f32)).astype(bf16)

    def pass_on(index, step):
        if index == 1:
            half_over(step).wait_recv()
        add(index, step)
        for member in range(2):
            back(index, step, member).start()

    def pass_all(index):
        loop(1, couples, lambda step: pass_on(index, step))
        if index == 1:
            half_over(0).wait_recv()
        add(index, 0)
        back(index, 0, 1 - me % 2).start()
        back_here(index).start()

    for part in range(PARTS + 1):
        for side in range(2):
            piece_over(part, side).wait_recv()
    pass_all(0)
    to_terms([d_gate, d_up], [0, 1], tensor, own_i)
    pass_all(1)
    factor(1, 1).wait_recv()
    factor(2, 1).start()

    def returned(index):
        back_here(index).wait()
        back_come(index, 0, 1 - me % 2).wait_recv()

        def come(step):
            for member in range(2):
                back_come(index, step, member).wait_recv()

        loop(1, couples, come)
        to = backs[index][3]
        for part in range(2):
            at = part * block + depth
            rest_of(to[:, at : at + LANES], ret_rest, part)
        return [
            jnp.concatenate(
                [
                    to[:, part * block : part * block + depth],
                    ret_rest[:, part * depth : (part + 1) * depth],
                ],
                axis=0,
            )
            for part in range(2)
        ]

    slices_landed(1)
    factor(0, 0).wait_recv()
    factor(2, 0).wait_recv()
    weight_grad(2)
    total = None
    for part, values in enumerate(returned(0)):
        at = slice(part * depth, (part + 1) * depth)
        layer_out[:, at] = dot(weighted[...], values).astype(bf16)
        term = dot(cotangent[:, at], values, INNER)
        total = term if total is None else total + term

    line = lax.broadcasted_iota(jnp.int32, (all_rows, LANES), 0)
    column = lax.broadcasted_iota(jnp.int32, (all_rows, LANES), 1)
    owner = jnp.where(line < count, line // TILE, line - count)
    to_owner = (owner == column).astype(f32).astype(bf16)
    left_over = total * select[...].astype(f32)
    sums = None
    for _ in range(3):
        term = left_over.astype(bf16)
        left_over = left_over - term.astype(f32)
        term = dot(term, to_owner)
        sums = term if sums is None else sums + term
    part_scores[...] = sums
    trade = remote(
        part_scores, other_scores, local_sems.at[7], local_sems.at[8], opposite
    )
    trade.start()

    factor(0, 1).wait_recv()
    factor(2, 1).wait_recv()
    for index in range(2):
        weight_grad(index)
    for part, values in enumerate(returned(1)):
        at = slice(part * depth, (part + 1) * depth)
        input_grad[:, at] = dot(select[...], values).astype(bf16)
    trade.wait()
    owner_scores[...] = part_scores[...] + other_scores[...]

    def spread_gone(matrix, part):
        swap(matrix, part).wait_send()
        for kind in range(3):
            spread(matrix, part, kind).wait_send()

    for matrix in range(3):
        loop(0, PARTS, lambda part, matrix=matrix: spread_gone(matrix, part))
    for kind in range(3):
        for late in range(2):
            factor(kind, late).wait_send()
    for part in range(PARTS + 1):
        for side in range(2):
            piece_over(part, side).wait_send()
    loop(0, couples, lambda step: half_over(step).wait_send())
    for index in range(2):
        loop(1, experts, lambda step, index=index: out_slab(index, step).wait_send())
        back(index, 0, 1 - me % 2).wait_send()

        def gone(step, index=index):
            for member in range(2):
                back(index, step, member).wait_send()

        loop(1, couples, gone)
        row_copy(index).wait_send()
        for kind in range(3):
            for copy in slice_copies(index, kind):
                copy.wait_send()


def layer(tokens, cotangent, select, weighted, weights, flag):
    experts, replicas, halves = (lax.axis_size(a) for a in ("expert", "dp", "tensor"))
    depth, units = weights[0].shape
    count, all_rows = experts * TILE, experts * CAP
    block, cells = depth + LANES, depth // LANES
    own_rows, half = tokens.shape

    def like(*shape, dtype=jnp.bfloat16):
        return jax.ShapeDtypeStruct(shape, dtype)

    def keep(*shape, dtype=jnp.bfloat16):
        return pltpu.VMEM(shape, dtype)

    out_shape = (
        like(own_rows, half),
        like(own_rows, half),
        like(own_rows, LANES, dtype=jnp.float32),
    ) + (like(depth, units),) * 3
    dma = pltpu.SemaphoreType.DMA
    return pl.pallas_call(
        functools.partial(layer_kernel, experts, replicas, halves),
        name="layer",
        out_shape=out_shape,
        in_specs=[WHOLE] * 4 + [ANY] * 3 + [WHOLE],
        out_specs=(WHOLE,) * len(out_shape),
        scratch_shapes=[keep(count, 2 * block)] * 2
        + [keep(halves, count, 2 * block)] * 2
        + [keep(experts, halves * half)] * 2
        + [keep(replicas * all_rows, depth)] * 2
        + [keep(replicas * count, LANES)] * 2
        + [keep(3, depth, units)]
        + [keep(replicas * depth, units)] * 3
        + [
            keep(3, all_rows, units, dtype=jnp.float32),
            keep(replicas * all_rows, 3 * units),
        ]
        + [keep(cells * experts, 2 * LANES)] * 3
        + [keep(count, 2 * block)] * 8
        + [keep(experts, half)]
        + [keep(own_rows, LANES, dtype=jnp.float32)] * 2
        + [
            dma((2, 2, experts)),
            dma((2, 2)),
            dma((2, 2, 4, 2)),
            dma((4, 3, PARTS, 2)),
            dma((2, experts // 2)),
            dma((2, 2 * PARTS + 2)),
            dma((2, 2, experts)),
            dma((2, 3, 2)),
            dma((9,)),
        ],
        compiler_params=pltpu.CompilerParams(
            collective_id=0, has_side_effects=True, vmem_limit_bytes=60 << 20
        ),
    )(tokens, cotangent, select, weighted, *weights, flag)


def copy_kernel(number, *refs):
    ins, outs, keeps, sems = (refs[:number], refs[number : 2 * number], refs[2 * number : -1], refs[-1])
    arrive = [
        pltpu.make_async_copy(ins[at], keeps[at], sems.at[0, at]) for at in range(number)
    ]
    leave = [
        pltpu.make_async_copy(keeps[at], outs[at], sems.at[1, at]) for at in range(number)
    ]
    for copy in arrive:
        copy.start()
    for first, second in zip(arrive, leave):
        first.wait()
        second.start()
    for copy in leave:
        copy.wait()


def copied(*arrays):
    number = len(arrays)
    return pl.pallas_call(
        functools.partial(copy_kernel, number),
        name="copy_out",
        out_shape=tuple(jax.ShapeDtypeStruct(a.shape, a.dtype) for a in arrays),
        in_specs=[ANY] * number,
        out_specs=(ANY,) * number,
        scratch_shapes=[pltpu.VMEM(a.shape, a.dtype) for a in arrays]
        + [pltpu.SemaphoreType.DMA((2, number))],
        compiler_params=pltpu.CompilerParams(vmem_limit_bytes=60 << 20),
    )(*arrays)


def on_device(tokens, routes, gates, cotangent, placement, swap_flag, w_gate, w_up, w_down):
    experts = lax.axis_size("expert")
    myself = lax.axis_index("expert")
    places = jnp.arange(experts, dtype=jnp.int32)
    partner = (places + experts // 2) % experts
    source = jnp.where(swap_flag == 1, partner, places)
    my_flag = jnp.sum(jnp.where(places == myself, swap_flag, 0)) == 1
    held = jnp.sum(jnp.where(source[:, None] == places[None, :], placement[None, :], 0), axis=1)
    tok_count, top_count = routes.shape
    slots_all = experts * CAP
    pair_owner = routes[:, :, None] == held[None, None, :]
    named = jnp.any(pair_owner, axis=1)
    gate_of = jnp.sum(jnp.where(pair_owner, gates[:, :, None].astype(jnp.float32), 0.0), axis=1)
    before = jnp.arange(tok_count)[:, None] > jnp.arange(tok_count)[None, :]
    earlier = jnp.dot(
        before.astype(jnp.bfloat16), named.astype(jnp.bfloat16), preferred_element_type=jnp.float32
    ).astype(jnp.int32)
    rank = jnp.where(named, earlier, CAP)
    column = jnp.arange(slots_all, dtype=jnp.int32)
    in_main = column < experts * TILE
    column_owner = jnp.where(in_main, column // TILE, column - experts * TILE)
    column_slot = jnp.where(in_main, column % TILE, TILE)
    spread = (places[:, None] == column_owner[None, :]).astype(jnp.bfloat16)
    column_rank = jnp.dot(rank.astype(jnp.bfloat16), spread, preferred_element_type=jnp.float32)
    match = column_rank == column_slot[None, :].astype(jnp.float32)
    select = match.astype(jnp.bfloat16)
    column_gate = jnp.dot(gate_of.astype(jnp.bfloat16), spread, preferred_element_type=jnp.float32)
    weighted = jnp.where(match, column_gate, 0.0).astype(jnp.bfloat16)
    flag = jnp.full((TILE, w_gate.shape[2]), my_flag, jnp.float32)
    layer_out, input_grad, owner_scores, *grads = layer(
        tokens, cotangent, select, weighted, (w_gate[0], w_up[0], w_down[0]), flag
    )
    gate_grad = jnp.sum(
        jnp.where(pair_owner, owner_scores[:, None, :experts], 0.0), axis=2
    )
    layer_out, input_grad, *grads = copied(layer_out, input_grad, *grads)
    return (layer_out, input_grad, gate_grad, *(grad[None] for grad in grads))


def solution(mesh):
    placed = (
        P(("expert", "dp"), "tensor"),
        P(("expert", "dp"), None),
        P(("expert", "dp"), None),
        P(("expert", "dp"), "tensor"),
        P(),
        P(),
        P("expert", "dp", "tensor"),
        P("expert", "dp", "tensor"),
        P("expert", "dp", "tensor"),
    )
    return jax.shard_map(
        on_device,
        mesh=mesh,
        in_specs=placed,
        out_specs=(
            P(("expert", "dp"), "tensor"),
            P(("expert", "dp"), "tensor"),
            P(("expert", "dp"), None),
            P("expert", "dp", "tensor"),
            P("expert", "dp", "tensor"),
            P("expert", "dp", "tensor"),
        ),
        check_vma=False,
    )
```
